128 devices in a mesh: wide: 32 (over z, y, core), narrow: 4 (over x).
Axes of the slice: x: 4, y: 4, z: 4, core: 2. Of those that a mesh axis runs over, the one named last changes fastest.
Arguments:
- tokens: bfloat16 [16384, 2048], P(('wide', 'narrow')), may hold values from -6 to 6
- expert_ids: int32 [16384, 10], P(('wide', 'narrow')), may hold values from 0 to 255, all different within a row; in each aligned block of 128 rows (0 to 127, 128 to 255, ...) at most 7 rows name the same one
- combine: int32 [16384, 10], P(('wide', 'narrow')), may hold values from 8 to 63
- w_gate: bfloat16 [256, 2048, 512], P(('wide', 'narrow')), may hold values from -0.125 to 0.125
- w_up: bfloat16 [256, 2048, 512], P(('wide', 'narrow')), may hold values from -0.125 to 0.125
- w_down: bfloat16 [256, 512, 2048], P(('wide', 'narrow')), may hold values from -0.25 to 0.25
- shared_gate_up: bfloat16 [2, 2048, 512], P(None, None, 'narrow'), may hold values from -0.125 to 0.125
- shared_down: bfloat16 [512, 2048], P('narrow'), may hold values from -0.25 to 0.25
- gate_vector: bfloat16 [2048], replicated, may hold values from -0.25 to 0.25
Outputs:
- layer_out: bfloat16 [16384, 2048], P(('wide', 'narrow'))
The draws below stay inside these ranges and needn't reach their ends.
Inputs may be any that keep to these rules, and one draw needn't show every extreme that they name: `expert_ids`: each row names 10 different experts. Among the 128 rows of one device no expert is named more than 7 times, and in every draw some device names some expert exactly 7 times. `combine`: an assignment's weight is its value divided by 256.
All inputs are finite; a program needn't handle non-finite values.
Results may differ from the reference program's by a relative error of at most 0.0054.
Values may be sent and summed in bfloat16 or wider, within the bound.
A program may use at most 128 MiB of HBM per device.

```python
import math
import jax
import jax.numpy as jnp
import numpy as np
from jax import lax

D = 2048
FF = 512
SH = 512
TOP = 10
EXPERTS = 256
TOK_DEV = 128
CAP = 7
TOKENS = 16384
DEVICES = 128


def touch_ends(result, rng, smallest, high):
    longest = result.shape.index(max(result.shape))
    spots = []
    for shift in (0, 1):
        where = [jax.random.randint(jax.random.fold_in(rng, axis), (), 0, length) for axis, length in enumerate(result.shape)]
        where[longest] = (where[longest] + shift) % result.shape[longest]
        spots.append(tuple(where))
    return result.at[spots[0]].set(smallest).at[spots[1]].set(high)


def block_scale(rng, shape, shards, least, top_value):
    def one(dim, shards_of):
        heights = jax.random.uniform(jax.random.fold_in(jax.random.fold_in(rng, 6), dim), (shards_of,), jnp.float32, least / len(shards), top_value / len(shards))
        return jnp.repeat(jnp.exp(heights), shape[dim] // shards_of).reshape((-1,) + (1,) * (len(shape) - dim - 1))

    factor_of = one(*shards[0])
    for cut in shards[1:]:
        factor_of = factor_of * one(*cut)
    return factor_of


def deal_out(key, own, number, rows, amount, top, bound, lean):
    sequence = jax.random.permutation(key, amount)
    packed, ordinary = portions_of(amount, rows * top, bound, lean, True), portions_of(amount, rows * top, bound, lean, False)
    places = jnp.arange(amount)

    def named(tallies, offset_by):
        used = int((tallies > 0).sum())
        fixed = max(1, used // 4)
        moved = fixed + (places - fixed + offset_by * (used - fixed)) % max(1, amount - fixed)
        return jnp.zeros((amount,), jnp.int32).at[sequence[jnp.where(places < fixed, places, moved)]].set(jnp.asarray(tallies, jnp.int32))

    tallies = jnp.where(number % 4 == 0, named(packed, number // 4), named(ordinary, number - number // 4 - 1))
    mixed = jax.random.permutation(jax.random.fold_in(own, 3), amount)
    source_of, taker = mixed[0:amount // 2 * 2:2], mixed[1:amount // 2 * 2:2]
    margin = jnp.minimum(tallies[source_of] - 1, bound - tallies[taker]) // 2
    margin = jnp.where((source_of == sequence[0]) | (taker == sequence[0]) | (tallies[taker] == 0), 0, jnp.maximum(margin, 0))
    moved = jax.random.randint(jax.random.fold_in(own, 4), (amount // 2,), 0, 1 << 20) % (margin + 1)
    tallies = tallies.at[source_of].add(-moved).at[taker].add(moved)
    items = jnp.searchsorted(jnp.cumsum(tallies), jnp.arange(rows * top), side="right").astype(jnp.int32)
    listing = items.reshape(top, rows).T
    listing = listing[jax.random.permutation(jax.random.fold_in(own, 1), rows)]
    offset_by = jax.random.randint(jax.random.fold_in(own, 2), (rows, 1), 0, top)
    return jnp.take_along_axis(listing, (jnp.arange(top)[None, :] + offset_by) % top, axis=1)


def portions_of(count, total, most, skew, full):
    loads = [(1 << 20) // math.isqrt(rank ** skew) + 1 for rank in range(1, count + 1)]
    largest = most if full else min(most, max(-(-total // count), total * loads[0] // sum(loads)))
    least = 1 if total - largest >= count - 1 else 0
    given, spare = [largest] + [least] * (count - 1), total - largest - least * (count - 1)
    while spare > 0:
        movable = [i for i in range(1, count) if given[i] < largest] or [i for i in range(1, count) if given[i] < most]
        mass, left = sum([loads[i] for i in movable]), spare
        for i in movable:
            extra = min(most - given[i], max(1, left * loads[i] // mass), spare)
            given[i] = given[i] + extra
            spare = spare - extra
    return np.array(given)


def noise(own_key, dims, scale, limit, split=(), held_as=jnp.bfloat16):
    values = jax.random.normal(own_key, dims, jnp.float32) * scale
    if len(split) > 0:
        values = block_scale(own_key, dims, split, -0.22, 0.18) * values
    return jnp.clip(values, min=-limit, max=limit).astype(held_as)


def setup_inputs(seed: int = 0) -> dict:
    key_of = jax.random.split(jax.random.key(seed), 10)
    tokens = noise(key_of[0], (TOKENS, D), 1.0, 6.0, ((0, 128),))
    expert_ids_keys = jax.random.split(jax.random.fold_in(key_of[1], 1), TOKENS // TOK_DEV)
    expert_ids_turns = jax.random.permutation(jax.random.fold_in(key_of[1], 3), TOKENS // TOK_DEV)
    expert_ids = jax.vmap(lambda own, number: deal_out(jax.random.fold_in(key_of[1], 2), own, number, TOK_DEV, EXPERTS, TOP, CAP, 2))(expert_ids_keys, expert_ids_turns).reshape((TOKENS, TOP))
    combine = touch_ends(jax.random.randint(key_of[2], (TOKENS, TOP), 8, 64), jax.random.fold_in(key_of[2], 1), 8, 63).astype(jnp.int32)
    w_gate = noise(key_of[3], (EXPERTS, D, FF), D ** -0.5, 0.125, ((0, 128),))
    w_up = noise(key_of[4], (EXPERTS, D, FF), D ** -0.5, 0.125, ((0, 128),))
    w_down = noise(key_of[5], (EXPERTS, FF, D), FF ** -0.5, 0.25, ((0, 128),))
    shared_gate_up = noise(key_of[6], (2, D, SH), D ** -0.5, 0.125, ((2, 4),))
    shared_down = noise(key_of[7], (SH, D), SH ** -0.5, 0.25, ((0, 4),))
    gate_vector = noise(key_of[8], (D,), (D // 4) ** -0.5, 0.25)
    return {"tokens": tokens, "expert_ids": expert_ids, "combine": combine, "w_gate": w_gate, "w_up": w_up, "w_down": w_down, "shared_gate_up": shared_gate_up, "shared_down": shared_down, "gate_vector": gate_vector}


def slot_order(flat_ids, experts_total):
    columns = jnp.arange(experts_total, dtype=jnp.int32)
    onehot = (flat_ids[:, None] == columns[None, :]).astype(jnp.int32)
    before = jnp.cumsum(onehot, axis=0) - onehot
    return jnp.sum(before * onehot, axis=1).astype(jnp.int32)


def place_block(block):
    return slot_order(block, EXPERTS)


def reference(tokens, expert_ids, combine, w_gate, w_up, w_down, shared_gate_up, shared_down, gate_vector):
    blocks = expert_ids.reshape(DEVICES, TOK_DEV * TOP).astype(jnp.int32)
    positions = lax.map(place_block, blocks)
    device_of = jnp.arange(DEVICES, dtype=jnp.int32)[:, None]
    slot_index = ((blocks * DEVICES + device_of) * CAP + positions).reshape(-1).astype(jnp.int32)
    within = jnp.arange(TOK_DEV * TOP, dtype=jnp.int32)[None, :] // TOP
    owners = (device_of * TOK_DEV + within).reshape(-1).astype(jnp.int32)
    slot_total = EXPERTS * DEVICES * CAP
    slot_token = jnp.full((slot_total,), -1, jnp.int32).at[slot_index].set(owners)
    slot_weight = jnp.zeros((slot_total,), jnp.float32).at[slot_index].set(
        combine.reshape(-1).astype(jnp.float32) / 256.0)
    span = DEVICES * CAP

    def expert_step(running, inputs):
        gate_w, up_w, down_w, expert = inputs
        token_rows = lax.dynamic_slice_in_dim(slot_token, (expert * span).astype(jnp.int32), span, 0)
        row_weights = lax.dynamic_slice_in_dim(slot_weight, (expert * span).astype(jnp.int32), span, 0)
        safe_rows = jnp.maximum(token_rows, 0)
        chosen = tokens[safe_rows]
        gate_part = jnp.dot(chosen, gate_w, preferred_element_type=jnp.float32)
        up_part = jnp.dot(chosen, up_w, preferred_element_type=jnp.float32)
        hidden = (jax.nn.silu(gate_part) * up_part).astype(jnp.bfloat16)
        produced = jnp.dot(hidden, down_w, preferred_element_type=jnp.float32).astype(jnp.bfloat16)
        running = running.at[safe_rows].add(row_weights[:, None] * produced.astype(jnp.float32))
        return running, None

    routed, unused = lax.scan(expert_step, jnp.zeros((TOKENS, D), jnp.float32),
                              (w_gate, w_up, w_down, jnp.arange(EXPERTS, dtype=jnp.int32)))
    shared_gate = jnp.dot(tokens, shared_gate_up[0], preferred_element_type=jnp.float32)
    shared_up = jnp.dot(tokens, shared_gate_up[1], preferred_element_type=jnp.float32)
    shared_hidden = (jax.nn.silu(shared_gate) * shared_up).astype(jnp.bfloat16)
    shared_out = jnp.dot(shared_hidden, shared_down, preferred_element_type=jnp.float32)
    shared_scale = jax.nn.sigmoid(jnp.dot(tokens, gate_vector, preferred_element_type=jnp.float32))
    return (routed + shared_scale[:, None] * shared_out).astype(jnp.bfloat16)
```

```python
import functools

import jax
import jax.numpy as jnp
from jax import lax
from jax.experimental import pallas as pl
from jax.experimental.pallas import tpu as pltpu
from jax.sharding import PartitionSpec as P

CAP = 7
MESH = pl.DeviceIdType.MESH
F32 = jnp.float32
BF16 = jnp.bfloat16


def grid_of(wide):
    side = 1
    while 2 * side * side < wide:
        side *= 2
    return wide // (2 * side), side


def offsets(wide):
    zs, ys = grid_of(wide)
    steps = [(dz, dy, dc) for dz in range(zs) for dy in range(ys) for dc in range(2)]
    steps = steps[1:]

    def far(step):
        dz, dy, dc = step
        return min(dz, zs - dz) + min(dy, ys - dy)

    return sorted(steps, key=lambda s: (-far(s), (s[0] + 2 * s[1]) % 4, s[2]))


def silu_product(gate, up):
    return gate * (1.0 / (1.0 + jnp.exp(-gate))) * up


def kernel(
    cfg,
    tok, meta, wg, wu, wd, sgu, sd, gv,
    out,
    T, metas, D, DT, O, X, Y, Wg, Wu, Wd, acc, H, Sg, Sd, Gv, shared, part, rs_out, rs_in, own,
    m_send, m_recv, t_send, t_recv, d_send, d_recv, y_send, y_recv, r_send, r_recv, loc, w_sem,
    own_sem, yown_sem, s_sem,
):
    wide, narrow, chunks, n, rows, model, ff, hid, top = cfg
    zs, ys = grid_of(wide)
    w = lax.axis_index("wide")
    nx = lax.axis_index("narrow")
    steps = offsets(wide)
    lanes = narrow * rows
    slots = wide * 8

    def peer(step):
        dz, dy, dc = step
        core = w % 2
        y = (w // 2) % ys
        z = w // (2 * ys)
        return (((z + dz) % zs) * ys + (y + dy) % ys) * 2 + (core + dc) % 2

    def near(k):
        return (nx + k) % narrow

    barrier = pltpu.get_barrier_semaphore()
    for k in range(1, narrow):
        pl.semaphore_signal(barrier, inc=1, device_id=(w, near(k)), device_id_type=MESH)
    for step in steps:
        pl.semaphore_signal(barrier, inc=1, device_id=(peer(step), nx), device_id_type=MESH)

    def weight_copy(which, c):
        cols = pl.ds(c * n, n)
        source = (wg.at[:, cols, :], wu.at[:, cols, :], wd.at[:, :, cols])[which]
        return pltpu.make_async_copy(source, (Wg, Wu, Wd)[which].at[c], w_sem.at[which, c])

    def own_tokens(c):
        return pltpu.make_async_copy(tok.at[:, pl.ds(c * n, n)], T.at[c, nx], loc.at[c])

    def small(which):
        target = (Sg, Sd, Gv, metas.at[nx])[which]
        return pltpu.make_async_copy((sgu, sd, gv, meta)[which], target, s_sem.at[which])

    for which in range(4):
        small(which).start()
    for c in range(chunks):
        own_tokens(c).start()

    pl.semaphore_wait(barrier, narrow - 1 + len(steps))

    def meta_copy(k):
        return pltpu.make_async_remote_copy(
            meta, metas.at[nx], m_send.at[k - 1], m_recv.at[k - 1],
            device_id=(w, near(k)), device_id_type=MESH)

    def token_copy(c, k):
        return pltpu.make_async_remote_copy(
            tok.at[:, pl.ds(c * n, n)], T.at[c, nx], t_send.at[c, k - 1], t_recv.at[c, k - 1],
            device_id=(w, near(k)), device_id_type=MESH)

    for k in range(1, narrow):
        meta_copy(k).start()
    for c in range(chunks):
        for k in range(1, narrow):
            token_copy(c, k).start()
    for c in range(chunks):
        for which in range(3):
            weight_copy(which, c).start()

    small(3).wait()
    for k in range(1, narrow):
        meta_copy(k).wait_recv()
    pair = lax.broadcasted_iota(jnp.int32, (2 * wide, rows), 0)
    expert = (pair // 2) * (2 * narrow) + 2 * nx + pair % 2
    before = (
        lax.broadcasted_iota(jnp.int32, (rows, rows), 0)
        < lax.broadcasted_iota(jnp.int32, (rows, rows), 1)
    ).astype(F32).astype(BF16)
    rho = lax.broadcasted_iota(jnp.int32, (slots, 2 * wide), 0)
    col = lax.broadcasted_iota(jnp.int32, (slots, 2 * wide), 1)
    pos_parts, weight_parts = [], []
    for s in range(narrow):
        chosen = jnp.zeros((2 * wide, rows), F32)
        weight = jnp.zeros((2 * wide, rows), F32)
        for k in range(top):
            ids = jnp.broadcast_to(metas[s, k:k + 1, :], (2 * wide, rows))
            mix = jnp.broadcast_to(metas[s, top + k:top + k + 1, :], (2 * wide, rows))
            hit = ids == expert
            chosen = jnp.where(hit, 1.0, chosen)
            weight = jnp.where(hit, mix.astype(F32) * (1.0 / 256.0), weight)
        rank = jnp.dot(chosen.astype(BF16), before, preferred_element_type=F32)
        place = jnp.where(chosen > 0.5, rank + 1.0, 0.0).astype(BF16)
        spread = (
            (col == (rho // 8) * 2 + rho % 2) & ((rho % 8) // 2 == s)
        ).astype(F32).astype(BF16)
        pos_parts.append(jnp.dot(spread, place, preferred_element_type=F32))
        weight_parts.append(jnp.dot(spread, weight.astype(BF16), preferred_element_type=F32))
    pos8 = jnp.concatenate(pos_parts, axis=1)
    w8 = jnp.concatenate(weight_parts, axis=1)
    for j in range(CAP):
        D[j] = jnp.where(pos8 == j + 1.0, 1.0, 0.0).astype(BF16)

    def block_copy(c, step):
        to = peer(step)
        return pltpu.make_async_remote_copy(
            O.at[c, :, to], X.at[c, :, w], d_send.at[c], d_recv.at[c],
            device_id=(to, nx), device_id_type=MESH)

    def own_block(c):
        return pltpu.make_async_copy(O.at[c, :, w], X.at[c, :, w], own_sem.at[c])

    def dispatch(c, carry):
        own_tokens(c).wait()
        for k in range(1, narrow):
            token_copy(c, k).wait_recv()
        tokens = T[c].reshape(lanes, n)

        def one(j, carry):
            O[c, j] = jnp.dot(D[j], tokens, preferred_element_type=F32).reshape(
                wide, 8, n).astype(BF16)
            return carry

        lax.fori_loop(0, CAP, one, 0)
        for step in steps:
            block_copy(c, step).start()
        own_block(c).start()
        return carry

    lax.fori_loop(0, chunks, dispatch, 0)

    for which in range(3):
        small(which).wait()
    shared[...] = jnp.zeros_like(shared)

    def shared_step(c, carry):
        tokens = T[c].reshape(lanes, n)
        at = pl.ds(pl.multiple_of(c * n, n), n)
        shared[0] += jnp.dot(tokens, Sg[0, at, :], preferred_element_type=F32)
        shared[1] += jnp.dot(tokens, Sg[1, at, :], preferred_element_type=F32)
        shared[2] += jnp.dot(tokens, Gv[at, :], preferred_element_type=F32)
        return carry

    lax.fori_loop(0, chunks, shared_step, 0)
    shared_hidden = silu_product(shared[0], shared[1]).astype(BF16)
    shared[2] = 1.0 / (1.0 + jnp.exp(-shared[2]))
    posT, wT = pos8.T, w8.T
    for j in range(CAP):
        DT[j] = jnp.where(posT == j + 1.0, wT, 0.0).astype(BF16)

    parity = lax.broadcasted_iota(jnp.int32, (slots, n), 0) % 2
    first = jnp.where(parity == 0, 1.0, 0.0).astype(BF16)
    second = jnp.where(parity == 1, 1.0, 0.0).astype(BF16)

    def all_but_own(buf, sem):
        view = buf.at[:, pl.ds(0, wide - 1)]
        return pltpu.make_async_copy(view, view, sem)

    acc[...] = jnp.zeros_like(acc)

    def up_step(c, carry):
        weight_copy(0, c).wait()
        weight_copy(1, c).wait()
        own_block(c).wait()
        all_but_own(X.at[c], d_recv.at[c]).wait()
        gate_w = Wg[c].reshape(2 * n, ff)
        up_w = Wu[c].reshape(2 * n, ff)

        def one(j, carry):
            x = X[c, j].reshape(slots, n)
            both = jnp.concatenate([x * first, x * second], axis=1)
            acc[j, :, :ff] += jnp.dot(both, gate_w, preferred_element_type=F32)
            acc[j, :, ff:] += jnp.dot(both, up_w, preferred_element_type=F32)
            return carry

        lax.fori_loop(0, CAP, one, 0)
        return carry

    lax.fori_loop(0, chunks, up_step, 0)

    parity_h = lax.broadcasted_iota(jnp.int32, (slots, ff), 0) % 2

    def hidden(j, carry):
        h = silu_product(acc[j, :, :ff], acc[j, :, ff:])
        H[j, :, :ff] = jnp.where(parity_h == 0, h, 0.0).astype(BF16)
        H[j, :, ff:] = jnp.where(parity_h == 1, h, 0.0).astype(BF16)
        return carry

    lax.fori_loop(0, CAP, hidden, 0)

    def back_copy(c, step):
        to = peer(step)
        return pltpu.make_async_remote_copy(
            X.at[c, :, to], Y.at[c, :, w], y_send.at[c], y_recv.at[c],
            device_id=(to, nx), device_id_type=MESH)

    def own_back(c):
        return pltpu.make_async_copy(X.at[c, :, w], Y.at[c, :, w], yown_sem.at[c])

    def down_step(c, carry):
        weight_copy(2, c).wait()
        down_w = Wd[c].reshape(2 * ff, n)

        def one(j, carry):
            X[c, j] = jnp.dot(H[j], down_w, preferred_element_type=F32).reshape(
                wide, 8, n).astype(BF16)
            return carry

        lax.fori_loop(0, CAP, one, 0)
        for step in steps:
            back_copy(c, step).start()
        own_back(c).start()
        return carry

    lax.fori_loop(0, chunks, down_step, 0)

    def sum_copy(c, k):
        return pltpu.make_async_remote_copy(
            rs_out.at[c, near(k)], rs_in.at[c, nx], r_send.at[c, k - 1], r_recv.at[c, k - 1],
            device_id=(w, near(k)), device_id_type=MESH)

    def combine(c, carry):
        own_back(c).wait()
        all_but_own(Y.at[c], y_recv.at[c]).wait()
        at = pl.ds(pl.multiple_of(c * n, n), n)
        scale = jnp.concatenate([shared[2]] * (n // 128), axis=1)
        part[...] = scale * jnp.dot(shared_hidden, Sd[:, at], preferred_element_type=F32)

        def one(j, carry):
            part[...] += jnp.dot(DT[j], Y[c, j].reshape(slots, n), preferred_element_type=F32)
            return carry

        lax.fori_loop(0, CAP, one, 0)
        rs_out[c] = part[...].reshape(narrow, rows, n).astype(BF16)
        for k in range(1, narrow):
            sum_copy(c, k).start()
        mine = pl.ds(pl.multiple_of(nx * rows, rows), rows)
        own[c] = part[mine, :]
        return carry

    lax.fori_loop(0, chunks, combine, 0)

    for c in range(chunks):
        total = own[c]
        for k in range(1, narrow):
            sum_copy(c, k).wait_recv()
        for k in range(1, narrow):
            total = total + rs_in[c, near(k)].astype(F32)
        out[:, c * n:(c + 1) * n] = total.astype(BF16)

    for k in range(1, narrow):
        meta_copy(k).wait_send()

    def drain(c, carry):
        for k in range(1, narrow):
            token_copy(c, k).wait_send()
            sum_copy(c, k).wait_send()
        all_but_own(O.at[c], d_send.at[c]).wait()
        all_but_own(X.at[c], y_send.at[c]).wait()
        return carry

    lax.fori_loop(0, chunks, drain, 0)


def on_device(chunks, tokens, expert_ids, combine, w_gate, w_up, w_down, gate_up, down, gate_vec):
    rows, model = tokens.shape
    top = expert_ids.shape[1]
    wide, narrow = lax.axis_size("wide"), lax.axis_size("narrow")
    ff, hid = w_gate.shape[2], down.shape[0]
    n = model // chunks
    slots = wide * 8
    lanes = narrow * rows
    meta = jnp.concatenate([expert_ids.T, combine.T], axis=0)
    meta = jnp.pad(meta, ((0, -meta.shape[0] % 8), (0, 0)))
    gv = jnp.broadcast_to(gate_vec[:, None], (model, 128))
    cfg = (wide, narrow, chunks, n, rows, model, ff, hid, top)
    any_spec = pl.BlockSpec(memory_space=pl.ANY)
    dma = pltpu.SemaphoreType.DMA
    return pl.pallas_call(
        functools.partial(kernel, cfg),
        out_shape=jax.ShapeDtypeStruct((rows, model), BF16),
        in_specs=[any_spec] * 8,
        out_specs=pl.BlockSpec(memory_space=pltpu.VMEM),
        scratch_shapes=[
            pltpu.VMEM((chunks, narrow, rows, n), BF16),
            pltpu.VMEM((narrow, *meta.shape), jnp.int32),
            pltpu.VMEM((CAP, slots, lanes), BF16),
            pltpu.VMEM((CAP, lanes, slots), BF16),
            pltpu.VMEM((chunks, CAP, wide, 8, n), BF16),
            pltpu.VMEM((chunks, CAP, wide, 8, n), BF16),
            pltpu.VMEM((chunks, CAP, wide, 8, n), BF16),
            pltpu.VMEM((chunks, 2, n, ff), BF16),
            pltpu.VMEM((chunks, 2, n, ff), BF16),
            pltpu.VMEM((chunks, 2, ff, n), BF16),
            pltpu.VMEM((CAP, slots, 2 * ff), F32),
            pltpu.VMEM((CAP, slots, 2 * ff), BF16),
            pltpu.VMEM((2, model, hid), BF16),
            pltpu.VMEM((hid, model), BF16),
            pltpu.VMEM((model, 128), BF16),
            pltpu.VMEM((3, lanes, hid), F32),
            pltpu.VMEM((lanes, n), F32),
            pltpu.VMEM((chunks, narrow, rows, n), BF16),
            pltpu.VMEM((chunks, narrow, rows, n), BF16),
            pltpu.VMEM((chunks, rows, n), F32),
            dma((narrow - 1,)), dma((narrow - 1,)),
            dma((chunks, narrow - 1)), dma((chunks, narrow - 1)),
            dma((chunks,)), dma((chunks,)),
            dma((chunks,)), dma((chunks,)),
            dma((chunks, narrow - 1)), dma((chunks, narrow - 1)),
            dma((chunks,)), dma((3, chunks)),
            dma((chunks,)), dma((chunks,)), dma((4,)),
        ],
        compiler_params=pltpu.CompilerParams(
            collective_id=0, has_side_effects=True, vmem_limit_bytes=66 * 1000 * 1000),
    )(tokens, meta, w_gate, w_up, w_down, gate_up, down, gv)


def solution(mesh, chunks=4):
    return jax.shard_map(
        functools.partial(on_device, chunks),
        mesh=mesh,
        in_specs=(
            P(("wide", "narrow"), None),
            P(("wide", "narrow"), None),
            P(("wide", "narrow"), None),
            P(("wide", "narrow"), None, None),
            P(("wide", "narrow"), None, None),
            P(("wide", "narrow"), None, None),
            P(None, None, "narrow"),
            P("narrow", None),
            P(),
        ),
        out_specs=P(("wide", "narrow"), None),
        check_vma=False,
    )
```

```python
import functools

import jax
import jax.numpy as jnp
from jax import lax
from jax.experimental import pallas as pl
from jax.experimental.pallas import tpu as pltpu
from jax.sharding import PartitionSpec as P

CAP = 7
MESH = pl.DeviceIdType.MESH
F32 = jnp.float32
BF16 = jnp.bfloat16


def grid_of(wide):
    side = 1
    while 2 * side * side < wide:
        side *= 2
    return wide // (2 * side), side


def offsets(wide):
    zs, ys = grid_of(wide)
    steps = [(dz, dy, dc) for dz in range(zs) for dy in range(ys) for dc in range(2)]
    steps = steps[1:]

    def far(step):
        dz, dy, dc = step
        return min(dz, zs - dz) + min(dy, ys - dy)

    return sorted(steps, key=lambda s: (-far(s), (s[0] + 2 * s[1]) % 4, s[2]))


def silu_product(gate, up):
    return gate * (1.0 / (1.0 + jnp.exp(-gate))) * up


def kernel(
    cfg,
    tok, ids_in, mix_in, wg, wu, wd, sgu, sd, gv,
    out,
    T, idv, mixv, D, DT, O, X, Y, Wg, Wu, Wd, acc, H, Sg, Sd, Gv, shared, part, rs_out, rs_in, own,
    m_send, m_recv, t_send, t_recv, d_send, d_recv, y_send, y_recv, r_send, r_recv, loc, w_sem,
    own_sem, yown_sem, s_sem,
):
    wide, narrow, chunks, n, rows, model, ff, hid, top = cfg
    zs, ys = grid_of(wide)
    w = lax.axis_index("wide")
    nx = lax.axis_index("narrow")
    steps = offsets(wide)
    lanes = narrow * rows
    slots = wide * 8

    def peer(step):
        dz, dy, dc = step
        core = w % 2
        y = (w // 2) % ys
        z = w // (2 * ys)
        return (((z + dz) % zs) * ys + (y + dy) % ys) * 2 + (core + dc) % 2

    def near(k):
        return (nx + k) % narrow

    barrier = pltpu.get_barrier_semaphore()
    for k in range(1, narrow):
        pl.semaphore_signal(barrier, inc=1, device_id=(w, near(k)), device_id_type=MESH)
    for step in steps:
        pl.semaphore_signal(barrier, inc=1, device_id=(peer(step), nx), device_id_type=MESH)

    def weight_copy(which, c):
        cols = pl.ds(c * n, n)
        source = (wg.at[:, cols, :], wu.at[:, cols, :], wd.at[:, :, cols])[which]
        return pltpu.make_async_copy(source, (Wg, Wu, Wd)[which].at[c], w_sem.at[which, c])

    def own_tokens(c):
        return pltpu.make_async_copy(tok.at[:, pl.ds(c * n, n)], T.at[c, nx], loc.at[c])

    def small(which):
        target = (Sg, Sd, Gv, idv.at[nx], mixv.at[nx])[which]
        return pltpu.make_async_copy((sgu, sd, gv, ids_in, mix_in)[which], target, s_sem.at[which])

    for which in range(5):
        small(which).start()
    for c in range(chunks):
        own_tokens(c).start()

    pl.semaphore_wait(barrier, narrow - 1 + len(steps))

    def meta_copy(which, k):
        source, target = ((ids_in, idv), (mix_in, mixv))[which]
        return pltpu.make_async_remote_copy(
            source, target.at[nx], m_send.at[which, k - 1], m_recv.at[which, k - 1],
            device_id=(w, near(k)), device_id_type=MESH)

    def token_copy(c, k):
        return pltpu.make_async_remote_copy(
            tok.at[:, pl.ds(c * n, n)], T.at[c, nx], t_send.at[c, k - 1], t_recv.at[c, k - 1],
            device_id=(w, near(k)), device_id_type=MESH)

    for k in range(1, narrow):
        meta_copy(0, k).start()
        meta_copy(1, k).start()
    for c in range(chunks):
        for k in range(1, narrow):
            token_copy(c, k).start()
    for c in range(chunks):
        for which in range(3):
            weight_copy(which, c).start()

    small(3).wait()
    small(4).wait()
    for k in range(1, narrow):
        meta_copy(0, k).wait_recv()
        meta_copy(1, k).wait_recv()
    pair = lax.broadcasted_iota(jnp.int32, (2 * wide, rows), 0)
    expert = (pair // 2) * (2 * narrow) + 2 * nx + pair % 2
    before = (
        lax.broadcasted_iota(jnp.int32, (rows, rows), 0)
        < lax.broadcasted_iota(jnp.int32, (rows, rows), 1)
    ).astype(F32).astype(BF16)
    rho = lax.broadcasted_iota(jnp.int32, (slots, wide * 2), 0)
    col = lax.broadcasted_iota(jnp.int32, (slots, wide * 2), 1)
    pos_parts, weight_parts = [[], []], [[], []]
    for s in range(narrow):
        chosen = jnp.zeros((2 * wide, rows), F32)
        weight = jnp.zeros((2 * wide, rows), F32)
        for k in range(top):
            ids = jnp.broadcast_to(idv[s, k:k + 1, :], (2 * wide, rows))
            mix = jnp.broadcast_to(mixv[s, k:k + 1, :], (2 * wide, rows))
            hit = ids == expert
            chosen = jnp.where(hit, 1.0, chosen)
            weight = jnp.where(hit, mix.astype(F32) * (1.0 / 256.0), weight)
        rank = jnp.dot(chosen.astype(BF16), before, preferred_element_type=F32)
        place = jnp.where(chosen > 0.5, rank + 1.0, 0.0).astype(BF16)
        weight = weight.astype(BF16)
        for e in range(2):
            spread = ((col == (rho // 8) * 2 + e) & (rho % 4 == s)).astype(F32).astype(BF16)
            pos_parts[e].append(jnp.dot(spread, place, preferred_element_type=F32))
            weight_parts[e].append(jnp.dot(spread, weight, preferred_element_type=F32))
    half = (lax.broadcasted_iota(jnp.int32, (slots, lanes), 0) % 8) // 4
    pos, mixes = [], []
    for e in range(2):
        found = jnp.concatenate(pos_parts[e], axis=1)
        pos.append(jnp.where(found > 0.5, found - half.astype(F32), -9.0))
        mixes.append(jnp.concatenate(weight_parts[e], axis=1))
    for g in range(CAP):
        D[g * slots:(g + 1) * slots, :] = jnp.where(
            (pos[0] == 2.0 * g + 1.0) | (pos[1] == 2.0 * g - 6.0), 1.0, 0.0).astype(BF16)

    def block_copy(c, step):
        to = peer(step)
        return pltpu.make_async_remote_copy(
            O.at[c, :, to], X.at[c, :, w], d_send.at[c], d_recv.at[c],
            device_id=(to, nx), device_id_type=MESH)

    def own_block(c):
        return pltpu.make_async_copy(O.at[c, :, w], X.at[c, :, w], own_sem.at[c])

    def dispatch(c, carry):
        own_tokens(c).wait()
        for k in range(1, narrow):
            token_copy(c, k).wait_recv()
        tokens = T[c].reshape(lanes, n)

        O[c] = jnp.dot(D[...], tokens, preferred_element_type=F32).reshape(
            CAP, wide, 8, n).astype(BF16)
        for step in steps:
            block_copy(c, step).start()
        own_block(c).start()
        return carry

    lax.fori_loop(0, chunks, dispatch, 0)

    for which in range(3):
        small(which).wait()
    shared[...] = jnp.zeros_like(shared)

    def shared_step(c, carry):
        tokens = T[c].reshape(lanes, n)
        at = pl.ds(pl.multiple_of(c * n, n), n)
        shared[0] += jnp.dot(tokens, Sg[0, at, :], preferred_element_type=F32)
        shared[1] += jnp.dot(tokens, Sg[1, at, :], preferred_element_type=F32)
        scored = tokens.astype(F32) * Gv[:, at].astype(F32)
        for q in range(n // 128):
            shared[2] += scored[:, q * 128:(q + 1) * 128]
        return carry

    lax.fori_loop(0, chunks, shared_step, 0)
    shared_hidden = silu_product(shared[0], shared[1]).astype(BF16)
    score = jnp.broadcast_to(jnp.sum(shared[2], axis=1, keepdims=True), (lanes, 128))
    shared[2] = 1.0 / (1.0 + jnp.exp(-score))
    pos_t, mix_t = [p.T for p in pos], [m.T for m in mixes]
    for g in range(CAP):
        DT[:, g * slots:(g + 1) * slots] = (
            jnp.where(pos_t[0] == 2.0 * g + 1.0, mix_t[0], 0.0)
            + jnp.where(pos_t[1] == 2.0 * g - 6.0, mix_t[1], 0.0)).astype(BF16)

    def all_but_own(buf, sem):
        view = buf.at[:, pl.ds(0, wide - 1)]
        return pltpu.make_async_copy(view, view, sem)

    acc[...] = jnp.zeros_like(acc)

    def up_step(c, carry):
        weight_copy(0, c).wait()
        weight_copy(1, c).wait()
        own_block(c).wait()
        all_but_own(X.at[c], d_recv.at[c]).wait()

        def one(e, carry):
            x = X[c, pl.ds(3 * e, 4)].reshape(4 * slots, n)
            acc[e, :, :ff] += jnp.dot(x, Wg[c, e], preferred_element_type=F32)
            acc[e, :, ff:] += jnp.dot(x, Wu[c, e], preferred_element_type=F32)
            return carry

        lax.fori_loop(0, 2, one, 0)
        return carry

    lax.fori_loop(0, chunks, up_step, 0)

    upper = (lax.broadcasted_iota(jnp.int32, (slots, ff), 0) % 8) // 4

    def hidden(g, carry):
        e, r = g // 4, g % 4
        at = pl.ds(pl.multiple_of(r * slots, slots), slots)
        h = silu_product(acc[e, at, :ff], acc[e, at, ff:])
        shared_row = (g == 3).astype(jnp.int32) - (g == 4).astype(jnp.int32)
        keep = shared_row * (2 * upper - 1) <= 0
        H[e, at, :] = jnp.where(keep, h, 0.0).astype(BF16)
        return carry

    lax.fori_loop(0, 8, hidden, 0)

    def back_copy(c, step):
        to = peer(step)
        return pltpu.make_async_remote_copy(
            X.at[c, :, to], Y.at[c, :, w], y_send.at[c], y_recv.at[c],
            device_id=(to, nx), device_id_type=MESH)

    def own_back(c):
        return pltpu.make_async_copy(X.at[c, :, w], Y.at[c, :, w], yown_sem.at[c])

    def down_step(c, carry):
        weight_copy(2, c).wait()
        low = jnp.dot(H[0], Wd[c, 0], preferred_element_type=F32)
        high = jnp.dot(H[1], Wd[c, 1], preferred_element_type=F32)
        X[c, 0:3] = low[:3 * slots].reshape(3, wide, 8, n).astype(BF16)
        X[c, 3] = (low[3 * slots:] + high[:slots]).reshape(wide, 8, n).astype(BF16)
        X[c, 4:7] = high[slots:].reshape(3, wide, 8, n).astype(BF16)
        for step in steps:
            back_copy(c, step).start()
        own_back(c).start()
        return carry

    lax.fori_loop(0, chunks, down_step, 0)

    def sum_copy(c, k):
        return pltpu.make_async_remote_copy(
            rs_out.at[c, near(k)], rs_in.at[c, nx], r_send.at[c, k - 1], r_recv.at[c, k - 1],
            device_id=(w, near(k)), device_id_type=MESH)

    def combine(c, carry):
        own_back(c).wait()
        all_but_own(Y.at[c], y_recv.at[c]).wait()
        at = pl.ds(pl.multiple_of(c * n, n), n)
        scale = jnp.concatenate([shared[2]] * (n // 128), axis=1)
        part[...] = scale * jnp.dot(shared_hidden, Sd[:, at], preferred_element_type=F32) + jnp.dot(
            DT[...], Y[c].reshape(CAP * slots, n), preferred_element_type=F32)
        rs_out[c] = part[...].reshape(narrow, rows, n).astype(BF16)
        for k in range(1, narrow):
            sum_copy(c, k).start()
        mine = pl.ds(pl.multiple_of(nx * rows, rows), rows)
        own[c] = part[mine, :]
        return carry

    lax.fori_loop(0, chunks, combine, 0)

    for c in range(chunks):
        total = own[c]
        for k in range(1, narrow):
            sum_copy(c, k).wait_recv()
        for k in range(1, narrow):
            total = total + rs_in[c, near(k)].astype(F32)
        out[:, c * n:(c + 1) * n] = total.astype(BF16)

    for k in range(1, narrow):
        meta_copy(0, k).wait_send()
        meta_copy(1, k).wait_send()

    def drain(c, carry):
        for k in range(1, narrow):
            token_copy(c, k).wait_send()
            sum_copy(c, k).wait_send()
        all_but_own(O.at[c], d_send.at[c]).wait()
        all_but_own(X.at[c], y_send.at[c]).wait()
        return carry

    lax.fori_loop(0, chunks, drain, 0)


def on_device(chunks, tokens, expert_ids, combine, w_gate, w_up, w_down, gate_up, down, gate_vec):
    rows, model = tokens.shape
    top = expert_ids.shape[1]
    wide, narrow = lax.axis_size("wide"), lax.axis_size("narrow")
    ff, hid = w_gate.shape[2], down.shape[0]
    n = model // chunks
    slots = wide * 8
    lanes = narrow * rows
    cfg = (wide, narrow, chunks, n, rows, model, ff, hid, top)
    any_spec = pl.BlockSpec(memory_space=pl.ANY)
    dma = pltpu.SemaphoreType.DMA
    return pl.pallas_call(
        functools.partial(kernel, cfg),
        out_shape=jax.ShapeDtypeStruct((rows, model), BF16),
        in_specs=[any_spec] * 9,
        out_specs=pl.BlockSpec(memory_space=pltpu.VMEM),
        scratch_shapes=[
            pltpu.VMEM((chunks, narrow, rows, n), BF16),
            pltpu.VMEM((narrow, top, rows), jnp.int32),
            pltpu.VMEM((narrow, top, rows), jnp.int32),
            pltpu.VMEM((CAP * slots, lanes), BF16),
            pltpu.VMEM((lanes, CAP * slots), BF16),
            pltpu.VMEM((chunks, CAP, wide, 8, n), BF16),
            pltpu.VMEM((chunks, CAP, wide, 8, n), BF16),
            pltpu.VMEM((chunks, CAP, wide, 8, n), BF16),
            pltpu.VMEM((chunks, 2, n, ff), BF16),
            pltpu.VMEM((chunks, 2, n, ff), BF16),
            pltpu.VMEM((chunks, 2, ff, n), BF16),
            pltpu.VMEM((2, 4 * slots, 2 * ff), F32),
            pltpu.VMEM((2, 4 * slots, ff), BF16),
            pltpu.VMEM((2, model, hid), BF16),
            pltpu.VMEM((hid, model), BF16),
            pltpu.VMEM((1, model), BF16),
            pltpu.VMEM((3, lanes, hid), F32),
            pltpu.VMEM((lanes, n), F32),
            pltpu.VMEM((chunks, narrow, rows, n), BF16),
            pltpu.VMEM((chunks, narrow, rows, n), BF16),
            pltpu.VMEM((chunks, rows, n), F32),
            dma((2, narrow - 1)), dma((2, narrow - 1)),
            dma((chunks, narrow - 1)), dma((chunks, narrow - 1)),
            dma((chunks,)), dma((chunks,)),
            dma((chunks,)), dma((chunks,)),
            dma((chunks, narrow - 1)), dma((chunks, narrow - 1)),
            dma((chunks,)), dma((3, chunks)),
            dma((chunks,)), dma((chunks,)), dma((5,)),
        ],
        compiler_params=pltpu.CompilerParams(
            collective_id=0, has_side_effects=True, vmem_limit_bytes=66 * 1000 * 1000),
    )(tokens, expert_ids.T, combine.T, w_gate, w_up, w_down, gate_up, down,
      gate_vec.reshape(1, model))


def solution(mesh, chunks=16):
    return jax.shard_map(
        functools.partial(on_device, chunks),
        mesh=mesh,
        in_specs=(
            P(("wide", "narrow"), None),
            P(("wide", "narrow"), None),
            P(("wide", "narrow"), None),
            P(("wide", "narrow"), None, None),
            P(("wide", "narrow"), None, None),
            P(("wide", "narrow"), None, None),
            P(None, None, "narrow"),
            P("narrow", None),
            P(),
        ),
        out_specs=P(("wide", "narrow"), None),
        check_vma=False,
    )
```

```python
import functools

import jax
import jax.numpy as jnp
from jax import lax
from jax.experimental import pallas as pl
from jax.experimental.pallas import tpu as pltpu
from jax.sharding import PartitionSpec as P

CAP = 7
MESH = pl.DeviceIdType.MESH
F32 = jnp.float32
BF16 = jnp.bfloat16


SIDE = 4
GROUP = 2 * SIDE * SIDE
KINDS = (0, 1, 0, 2)


def offsets():
    steps = [(da, db, dc) for da in range(SIDE) for db in range(SIDE) for dc in range(2)]
    steps = steps[1:]

    def far(step):
        return min(step[0], SIDE - step[0]) + min(step[1], SIDE - step[1])

    return sorted(steps, key=lambda s: (-far(s), (s[0] + 2 * s[1]) % 4, s[2]))


def silu_product(gate, up):
    return gate * (1.0 / (1.0 + jnp.exp(-gate))) * up


def kernel(
    cfg,
    tok, ids_in, mix_in, wg, wu, wd, sgu, sd, gv,
    out,
    T, TO, idv, mixv, D, O, X, Y, Wg, Wu, Wd, acc, H, Sg, Sd, Gv, shared, rs_out, rs_in,
    sh_out, sh_in, own,
    m_send, m_recv, t_send, t_recv, to_send, to_recv, d_send, d_recv, y_send, y_recv,
    r_send, r_recv, s_send, s_recv, loc, loco, w_sem, own_sem, yown_sem, small_sem,
):
    chunks, n, rows, model, ff, hid, top = cfg
    w = lax.axis_index("wide")
    x = lax.axis_index("narrow")
    core, y, z = w % 2, (w // 2) % SIDE, w // (2 * SIDE)
    at = (x, y, z)
    rounds, pairs = chunks // 4, chunks // 2
    lanes = SIDE * rows
    slots = GROUP * 8
    steps = offsets()

    def device(xx, yy, zz, cc):
        return ((zz * SIDE + yy) * 2 + cc, xx)

    def place(p):
        first, second = ((z, y), (z, x), (x, y))[p]
        return (first * SIDE + second) * 2 + core

    def far_peer(p, step):
        da, db, dc = step
        first, second = ((z, y), (z, x), (x, y))[p]
        first, second, cc = (first + da) % SIDE, (second + db) % SIDE, (core + dc) % 2
        spot = ((x, second, first), (second, y, first), (first, second, z))[p]
        return (first * SIDE + second) * 2 + cc, device(*spot, cc)

    def near(p, k):
        other = (at[p] + k) % SIDE
        spot = tuple(other if q == p else at[q] for q in range(3))
        return other, device(*spot, core)

    barrier = pltpu.get_barrier_semaphore()
    greeted = 0
    for dx in range(SIDE):
        for dy in range(SIDE):
            for dz in range(SIDE):
                for dc in range(2):
                    if dx * dy * dz == 0 and (dx, dy, dz, dc) != (0, 0, 0, 0):
                        greeted += 1
                        pl.semaphore_signal(
                            barrier, inc=1,
                            device_id=device((x + dx) % SIDE, (y + dy) % SIDE, (z + dz) % SIDE,
                                             (core + dc) % 2),
                            device_id_type=MESH)

    def weight_copy(which, m):
        cols = pl.ds(m * 2 * n, 2 * n)
        source = (wg.at[:, cols, :], wu.at[:, cols, :], wd.at[:, :, cols])[which]
        return pltpu.make_async_copy(source, (Wg, Wu, Wd)[which].at[m], w_sem.at[which, m])

    def own_tokens(c):
        return pltpu.make_async_copy(tok.at[:, pl.ds(c * n, n)], T.at[c, x], loc.at[c])

    def own_tokens_other(p, r):
        c = r * 4 + KINDS.index(p)
        return pltpu.make_async_copy(
            tok.at[:, pl.ds(c * n, n)], TO.at[p - 1, r, at[p]], loco.at[p - 1, r])

    def small(which):
        source = (sgu, sd, gv)[which]
        return pltpu.make_async_copy(source, (Sg, Sd, Gv)[which], small_sem.at[which])

    def own_meta(which, p):
        source, target = ((ids_in, idv), (mix_in, mixv))[which]
        return pltpu.make_async_copy(
            source, target.at[p, at[p]], small_sem.at[3 + which * 3 + p])

    for p in range(3):
        own_meta(0, p).start()
        own_meta(1, p).start()
    for c in range(chunks):
        own_tokens(c).start()
    for r in range(rounds):
        own_tokens_other(1, r).start()
        own_tokens_other(2, r).start()
    for which in range(3):
        small(which).start()

    pl.semaphore_wait(barrier, greeted)

    def meta_copy(which, p, k):
        source, target = ((ids_in, idv), (mix_in, mixv))[which]
        return pltpu.make_async_remote_copy(
            source, target.at[p, at[p]], m_send.at[which, p, k - 1], m_recv.at[which, p, k - 1],
            device_id=near(p, k)[1], device_id_type=MESH)

    def token_copy(c, k):
        return pltpu.make_async_remote_copy(
            tok.at[:, pl.ds(c * n, n)], T.at[c, x], t_send.at[c, k - 1], t_recv.at[c, k - 1],
            device_id=near(0, k)[1], device_id_type=MESH)

    def token_copy_other(p, r, k):
        c = r * 4 + KINDS.index(p)
        return pltpu.make_async_remote_copy(
            tok.at[:, pl.ds(c * n, n)], TO.at[p - 1, r, at[p]],
            to_send.at[p - 1, r, k - 1], to_recv.at[p - 1, r, k - 1],
            device_id=near(p, k)[1], device_id_type=MESH)

    for p in range(3):
        for k in range(1, SIDE):
            meta_copy(0, p, k).start()
            meta_copy(1, p, k).start()
    for r in range(rounds):
        for q, p in enumerate(KINDS):
            for k in range(1, SIDE):
                if p == 0:
                    token_copy(r * 4 + q, k).start()
                else:
                    token_copy_other(p, r, k).start()
    for m in range(pairs):
        for which in range(3):
            weight_copy(which, m).start()

    for p in range(3):
        for which in range(2):
            own_meta(which, p).wait()
            for k in range(1, SIDE):
                meta_copy(which, p, k).wait_recv()
    pair = lax.broadcasted_iota(jnp.int32, (2 * GROUP, rows), 0)
    before = (
        lax.broadcasted_iota(jnp.int32, (rows, rows), 0)
        < lax.broadcasted_iota(jnp.int32, (rows, rows), 1)
    ).astype(F32).astype(BF16)
    rho = lax.broadcasted_iota(jnp.int32, (slots, 2 * GROUP), 0)
    col = lax.broadcasted_iota(jnp.int32, (slots, 2 * GROUP), 1)
    half = ((lax.broadcasted_iota(jnp.int32, (slots, lanes), 0) % 8) // 4).astype(F32)

    def slot_tables(p):
        by_first = jnp.where(p == 2, 2, 64)
        by_second = jnp.where(p == 1, 2, 16)
        base = jnp.where(p == 0, 2 * x, jnp.where(p == 1, 16 * y, 64 * z))
        expert = (
            base + (pair // 16) * by_first + ((pair // 4) % 4) * by_second
            + ((pair // 2) % 2) * 8 + pair % 2)
        pos_parts, weight_parts = [[], []], [[], []]
        for s in range(SIDE):
            chosen = jnp.zeros((2 * GROUP, rows), F32)
            weight = jnp.zeros((2 * GROUP, rows), F32)
            for k in range(top):
                ids = jnp.broadcast_to(idv[p, s, k:k + 1, :], (2 * GROUP, rows))
                mix = jnp.broadcast_to(mixv[p, s, k:k + 1, :], (2 * GROUP, rows))
                hit = ids == expert
                chosen = jnp.where(hit, 1.0, chosen)
                weight = jnp.where(hit, mix.astype(F32) * (1.0 / 256.0), weight)
            rank = jnp.dot(chosen.astype(BF16), before, preferred_element_type=F32)
            spot = jnp.where(chosen > 0.5, rank + 1.0, 0.0).astype(BF16)
            weight = weight.astype(BF16)
            for e in range(2):
                spread = ((col == (rho // 8) * 2 + e) & (rho % 4 == s)).astype(F32).astype(BF16)
                pos_parts[e].append(jnp.dot(spread, spot, preferred_element_type=F32))
                weight_parts[e].append(jnp.dot(spread, weight, preferred_element_type=F32))
        pos, mixes = [], []
        for e in range(2):
            found = jnp.concatenate(pos_parts[e], axis=1)
            pos.append(jnp.where(found > 0.5, found - half, -9.0))
            mixes.append(jnp.concatenate(weight_parts[e], axis=1))
        return pos, mixes

    def pick_table(p, carry):
        pos, mixes = slot_tables(p)
        for g in range(CAP):
            hot = jnp.where(
                (pos[0] == 2.0 * g + 1.0) | (pos[1] == 2.0 * g - 6.0), 1.0, 0.0).astype(BF16)
            for q in range(lanes // 128):
                D[p, g * (lanes // 128) + q] = hot[:, q * 128:(q + 1) * 128]
        return carry

    lax.fori_loop(0, 3, pick_table, 0)

    def block_copy(p, c, step):
        spot, to = far_peer(p, step)
        return pltpu.make_async_remote_copy(
            O.at[c, :, spot], X.at[c, :, place(p)], d_send.at[c], d_recv.at[c],
            device_id=to, device_id_type=MESH)

    def own_block(p, c):
        return pltpu.make_async_copy(O.at[c, :, place(p)], X.at[c, :, place(p)], own_sem.at[c])

    def dispatch(r, carry):
        for q, p in enumerate(KINDS):
            c = r * 4 + q
            if p == 0:
                own_tokens(c).wait()
                for k in range(1, SIDE):
                    token_copy(c, k).wait_recv()
                tokens = T[c].reshape(lanes, n)
            else:
                own_tokens_other(p, r).wait()
                for k in range(1, SIDE):
                    token_copy_other(p, r, k).wait_recv()
                tokens = TO[p - 1, r].reshape(lanes, n)
            cut = lanes // 128
            picks = jnp.concatenate(
                [jnp.concatenate([D[p, g * cut + b] for b in range(cut)], axis=1)
                 for g in range(CAP)], axis=0)
            O[c] = jnp.dot(picks, tokens, preferred_element_type=F32).reshape(
                CAP, GROUP, 8, n).astype(BF16)
            for step in steps:
                block_copy(p, c, step).start()
            own_block(p, c).start()
        return carry

    lax.fori_loop(0, rounds, dispatch, 0)
    for r in range(rounds):
        for q, p in enumerate(KINDS):
            if p != 0:
                for k in range(1, SIDE):
                    token_copy(r * 4 + q, k).start()

    def sum_table(p, carry):
        pos, mixes = slot_tables(p)
        pos_t, mix_t = [v.T for v in pos], [v.T for v in mixes]
        for g in range(CAP):
            block = (jnp.where(pos_t[0] == 2.0 * g + 1.0, mix_t[0], 0.0)
                     + jnp.where(pos_t[1] == 2.0 * g - 6.0, mix_t[1], 0.0)).astype(BF16)
            for b in range(2):
                D[p, pl.ds((2 * g + b) * 2, 2)] = block[:, b * 128:(b + 1) * 128].reshape(
                    2, lanes // 2, 128)
        return carry

    lax.fori_loop(0, 3, sum_table, 0)
    acc[...] = jnp.zeros_like(acc)

    here = lax.broadcasted_iota(jnp.int32, (slots, slots), 0)
    there = lax.broadcasted_iota(jnp.int32, (slots, slots), 1)

    def reorder(p):
        scale = 16 if p == 1 else 64
        low, high = there % 4, (there // scale) % 4
        moved = there + (high - low) + (low - high) * scale
        return (here == moved).astype(F32).astype(BF16)

    def all_but_own(buf, sem):
        view = buf.at[:, pl.ds(0, GROUP - 1)]
        return pltpu.make_async_copy(view, view, sem)

    def up_step(r, carry):
        for b in range(2):
            m = 2 * r + b
            weight_copy(0, m).wait()
            weight_copy(1, m).wait()
            for q in (2 * b, 2 * b + 1):
                own_block(KINDS[q], r * 4 + q).wait()
                all_but_own(X.at[r * 4 + q], d_recv.at[r * 4 + q]).wait()
            p = KINDS[2 * b + 1]
            c = r * 4 + 2 * b
            straight = [X[c, g].reshape(slots, n) for g in range(CAP)]
            mixed = jnp.concatenate([X[c + 1, g].reshape(slots, n) for g in range(CAP)], axis=1)
            mixed = jnp.dot(reorder(p), mixed, preferred_element_type=F32).astype(BF16)
            both = [
                jnp.concatenate([straight[g], mixed[:, g * n:(g + 1) * n]], axis=1)
                for g in range(CAP)]
            for e in range(2):
                v = jnp.concatenate(both[3 * e:3 * e + 4], axis=0)
                acc[e, :, :ff] += jnp.dot(v, Wg[m, e], preferred_element_type=F32)
                acc[e, :, ff:] += jnp.dot(v, Wu[m, e], preferred_element_type=F32)
        return carry

    lax.fori_loop(0, rounds, up_step, 0)

    upper = (lax.broadcasted_iota(jnp.int32, (slots, ff), 0) % 8) // 4

    def hidden(g, carry):
        e, b = g // 4, g % 4
        part = pl.ds(pl.multiple_of(b * slots, slots), slots)
        h = silu_product(acc[e, part, :ff], acc[e, part, ff:])
        mixed_row = (g == 3).astype(jnp.int32) - (g == 4).astype(jnp.int32)
        keep = mixed_row * (2 * upper - 1) <= 0
        H[e, part, :] = jnp.where(keep, h, 0.0).astype(BF16)
        return carry

    lax.fori_loop(0, 8, hidden, 0)

    def back_copy(p, c, step):
        spot, to = far_peer(p, step)
        return pltpu.make_async_remote_copy(
            X.at[c, :, spot], Y.at[c, :, place(p)], y_send.at[c], y_recv.at[c],
            device_id=to, device_id_type=MESH)

    def own_back(p, c):
        return pltpu.make_async_copy(X.at[c, :, place(p)], Y.at[c, :, place(p)], yown_sem.at[c])

    def down_step(r, carry):
        for b in range(2):
            m = 2 * r + b
            weight_copy(2, m).wait()
            low = jnp.dot(H[0], Wd[m, 0], preferred_element_type=F32)
            high = jnp.dot(H[1], Wd[m, 1], preferred_element_type=F32)
            made = [low[g * slots:(g + 1) * slots] for g in range(3)]
            made.append(low[3 * slots:] + high[:slots])
            made += [high[g * slots:(g + 1) * slots] for g in range(1, 4)]
            c = r * 4 + 2 * b
            for g in range(CAP):
                X[c, g] = made[g][:, :n].reshape(GROUP, 8, n).astype(BF16)
            for step in steps:
                back_copy(0, c, step).start()
            own_back(0, c).start()
            p = KINDS[2 * b + 1]
            mixed = jnp.concatenate([v[:, n:].astype(BF16) for v in made], axis=1)
            mixed = jnp.dot(reorder(p), mixed, preferred_element_type=F32)
            for g in range(CAP):
                X[c + 1, g] = mixed[:, g * n:(g + 1) * n].reshape(GROUP, 8, n).astype(BF16)
            for step in steps:
                back_copy(p, c + 1, step).start()
            own_back(p, c + 1).start()
        return carry

    lax.fori_loop(0, rounds, down_step, 0)

    for which in range(3):
        small(which).wait()
    for r in range(rounds):
        for q, p in enumerate(KINDS):
            if p != 0:
                own_tokens(r * 4 + q).wait()
                for k in range(1, SIDE):
                    token_copy(r * 4 + q, k).wait_recv()
    shared[...] = jnp.zeros_like(shared)

    def shared_step(c, carry):
        tokens = T[c].reshape(lanes, n)
        span = pl.ds(pl.multiple_of(c * n, n), n)
        shared[0] += jnp.dot(tokens, Sg[0, span, :], preferred_element_type=F32)
        shared[1] += jnp.dot(tokens, Sg[1, span, :], preferred_element_type=F32)
        scored = tokens.astype(F32) * Gv[:, span].astype(F32)
        for q in range(n // 128):
            shared[2] += scored[:, q * 128:(q + 1) * 128]
        return carry

    lax.fori_loop(0, chunks, shared_step, 0)
    shared_hidden = silu_product(shared[0], shared[1]).astype(BF16)
    score = jnp.broadcast_to(jnp.sum(shared[2], axis=1, keepdims=True), (lanes, 128))
    shared[2] = 1.0 / (1.0 + jnp.exp(-score))

    def shared_part(c):
        span = pl.ds(pl.multiple_of(c * n, n), n)
        scale = jnp.concatenate([shared[2]] * (n // 128), axis=1)
        return scale * jnp.dot(shared_hidden, Sd[:, span], preferred_element_type=F32)

    def sum_copy(p, c, k):
        other, to = near(p, k)
        return pltpu.make_async_remote_copy(
            rs_out.at[c, other], rs_in.at[c, at[p]], r_send.at[c, k - 1], r_recv.at[c, k - 1],
            device_id=to, device_id_type=MESH)

    def shared_copy(m, k):
        other, to = near(0, k)
        return pltpu.make_async_remote_copy(
            sh_out.at[m, other], sh_in.at[m, x], s_send.at[m, k - 1], s_recv.at[m, k - 1],
            device_id=to, device_id_type=MESH)

    def shared_sums(m, carry):
        sh_out[m] = shared_part(2 * m + 1).reshape(SIDE, rows, n).astype(BF16)
        for k in range(1, SIDE):
            shared_copy(m, k).start()
        return carry

    lax.fori_loop(0, pairs, shared_sums, 0)

    def combine(r, carry):
        for q, p in enumerate(KINDS):
            c = r * 4 + q
            own_back(p, c).wait()
            all_but_own(Y.at[c], y_recv.at[c]).wait()
            table = jnp.concatenate(
                [D[p, 2 * b:2 * b + 2].reshape(lanes, 128) for b in range(2 * CAP)], axis=1)
            part = jnp.dot(
                table, Y[c].reshape(CAP * slots, n), preferred_element_type=F32)
            if p == 0:
                part = part + shared_part(c)
            own[...] = part.reshape(SIDE, rows, n)
            rs_out[c] = own[...].astype(BF16)
            for k in range(1, SIDE):
                sum_copy(p, c, k).start()
        return carry

    lax.fori_loop(0, rounds, combine, 0)

    def finish(r, carry):
        for q, p in enumerate(KINDS):
            c = r * 4 + q
            for k in range(1, SIDE):
                sum_copy(p, c, k).wait_recv()
            total = rs_out[c, at[p]].astype(F32)
            for k in range(1, SIDE):
                total = total + rs_in[c, near(p, k)[0]].astype(F32)
            if p != 0:
                m = c // 2
                for k in range(1, SIDE):
                    shared_copy(m, k).wait_recv()
                total = total + sh_out[m, x].astype(F32)
                for k in range(1, SIDE):
                    total = total + sh_in[m, near(0, k)[0]].astype(F32)
            out[:, pl.ds(pl.multiple_of(c * n, n), n)] = total.astype(BF16)
        return carry

    lax.fori_loop(0, rounds, finish, 0)

    for p in range(3):
        for k in range(1, SIDE):
            meta_copy(0, p, k).wait_send()
            meta_copy(1, p, k).wait_send()

    def drain(r, carry):
        for q, p in enumerate(KINDS):
            c = r * 4 + q
            for k in range(1, SIDE):
                token_copy(c, k).wait_send()
                sum_copy(p, c, k).wait_send()
                if p != 0:
                    token_copy_other(p, r, k).wait_send()
                    shared_copy(c // 2, k).wait_send()
            all_but_own(O.at[c], d_send.at[c]).wait()
            all_but_own(X.at[c], y_send.at[c]).wait()
        return carry

    lax.fori_loop(0, rounds, drain, 0)


def on_device(chunks, tokens, expert_ids, combine, w_gate, w_up, w_down, gate_up, down, gate_vec):
    rows, model = tokens.shape
    top = expert_ids.shape[1]
    ff, hid = w_gate.shape[2], down.shape[0]
    n = model // chunks
    slots = GROUP * 8
    lanes = SIDE * rows
    rounds, pairs = chunks // 4, chunks // 2
    near = SIDE - 1
    cfg = (chunks, n, rows, model, ff, hid, top)
    any_spec = pl.BlockSpec(memory_space=pl.ANY)
    dma = pltpu.SemaphoreType.DMA
    return pl.pallas_call(
        functools.partial(kernel, cfg),
        out_shape=jax.ShapeDtypeStruct((rows, model), BF16),
        in_specs=[any_spec] * 9,
        out_specs=pl.BlockSpec(memory_space=pltpu.VMEM),
        scratch_shapes=[
            pltpu.VMEM((chunks, SIDE, rows, n), BF16),
            pltpu.VMEM((2, rounds, SIDE, rows, n), BF16),
            pltpu.VMEM((3, SIDE, top, rows), jnp.int32),
            pltpu.VMEM((3, SIDE, top, rows), jnp.int32),
            pltpu.VMEM((3, 4 * CAP, 256, 128), BF16),
            pltpu.VMEM((chunks, CAP, GROUP, 8, n), BF16),
            pltpu.VMEM((chunks, CAP, GROUP, 8, n), BF16),
            pltpu.VMEM((chunks, CAP, GROUP, 8, n), BF16),
            pltpu.VMEM((pairs, 2, 2 * n, ff), BF16),
            pltpu.VMEM((pairs, 2, 2 * n, ff), BF16),
            pltpu.VMEM((pairs, 2, ff, 2 * n), BF16),
            pltpu.VMEM((2, 4 * slots, 2 * ff), F32),
            pltpu.VMEM((2, 4 * slots, ff), BF16),
            pltpu.VMEM((2, model, hid), BF16),
            pltpu.VMEM((hid, model), BF16),
            pltpu.VMEM((1, model), BF16),
            pltpu.VMEM((3, lanes, hid), F32),
            pltpu.VMEM((chunks, SIDE, rows, n), BF16),
            pltpu.VMEM((chunks, SIDE, rows, n), BF16),
            pltpu.VMEM((pairs, SIDE, rows, n), BF16),
            pltpu.VMEM((pairs, SIDE, rows, n), BF16),
            pltpu.VMEM((SIDE, rows, n), F32),
            dma((2, 3, near)), dma((2, 3, near)),
            dma((chunks, near)), dma((chunks, near)),
            dma((2, rounds, near)), dma((2, rounds, near)),
            dma((chunks,)), dma((chunks,)),
            dma((chunks,)), dma((chunks,)),
            dma((chunks, near)), dma((chunks, near)),
            dma((pairs, near)), dma((pairs, near)),
            dma((chunks,)), dma((2, rounds)), dma((3, pairs)),
            dma((chunks,)), dma((chunks,)), dma((9,)),
        ],
        compiler_params=pltpu.CompilerParams(
            collective_id=0, has_side_effects=True, vmem_limit_bytes=67043328),
    )(tokens, expert_ids.T, combine.T, w_gate, w_up, w_down, gate_up, down,
      gate_vec.reshape(1, model))


def solution(mesh, chunks=16):
    return jax.shard_map(
        functools.partial(on_device, chunks),
        mesh=mesh,
        in_specs=(
            P(("wide", "narrow"), None),
            P(("wide", "narrow"), None),
            P(("wide", "narrow"), None),
            P(("wide", "narrow"), None, None),
            P(("wide", "narrow"), None, None),
            P(("wide", "narrow"), None, None),
            P(None, None, "narrow"),
            P("narrow", None),
            P(),
        ),
        out_specs=P(("wide", "narrow"), None),
        check_vma=False,
    )
```

```python
import functools

import jax
import jax.numpy as jnp
from jax import lax
from jax.experimental import pallas as pl
from jax.experimental.pallas import tpu as pltpu
from jax.sharding import PartitionSpec as P

CAP = 7
MESH = pl.DeviceIdType.MESH
F32 = jnp.float32
BF16 = jnp.bfloat16


SIDE = 4
GROUP = 2 * SIDE * SIDE
KINDS = (0, 1, 0, 2)
OUTWARD = ((0, 4), (4, 3))
HOMEWARD = ((0, 3), (3, 4))


def offsets():
    steps = [(da, db, dc) for da in range(SIDE) for db in range(SIDE) for dc in range(2)]
    steps = steps[1:]

    def far(step):
        return min(step[0], SIDE - step[0]) + min(step[1], SIDE - step[1])

    return sorted(steps, key=lambda s: (-far(s), (s[0] + 2 * s[1]) % 4, s[2]))


def silu_product(gate, up):
    return gate * (1.0 / (1.0 + jnp.exp(-gate))) * up


def kernel(
    cfg,
    tok, ids_in, mix_in, wg, wu, wd, sgu, sd, gv,
    out,
    T, TO, idv, mixv, D, O, X, Y, Wg, Wu, Wd, acc, H, Sg, Sd, Gv, shared, rs_in, sh_in,
    m_send, m_recv, t_send, t_recv, to_send, to_recv, d_send, d_recv, y_send, y_recv,
    r_send, r_recv, s_send, s_recv, loc, loco, w_sem, own_sem, yown_sem, small_sem,
):
    chunks, n, rows, model, ff, hid, top = cfg
    w = lax.axis_index("wide")
    x = lax.axis_index("narrow")
    core, y, z = w % 2, (w // 2) % SIDE, w // (2 * SIDE)
    at = (x, y, z)
    rounds, pairs = chunks // 4, chunks // 2
    lanes = SIDE * rows
    slots = GROUP * 8
    steps = offsets()

    def device(xx, yy, zz, cc):
        return ((zz * SIDE + yy) * 2 + cc, xx)

    def place(p):
        first, second = ((z, y), (z, x), (x, y))[p]
        return (first * SIDE + second) * 2 + core

    def far_peer(p, step):
        da, db, dc = step
        first, second = ((z, y), (z, x), (x, y))[p]
        first, second, cc = (first + da) % SIDE, (second + db) % SIDE, (core + dc) % 2
        spot = ((x, second, first), (second, y, first), (first, second, z))[p]
        return (first * SIDE + second) * 2 + cc, device(*spot, cc)

    def near(p, k):
        other = (at[p] + k) % SIDE
        spot = tuple(other if q == p else at[q] for q in range(3))
        return other, device(*spot, core)

    barrier = pltpu.get_barrier_semaphore()
    greeted = 0
    for dx in range(SIDE):
        for dy in range(SIDE):
            for dz in range(SIDE):
                for dc in range(2):
                    if dx * dy * dz == 0 and (dx, dy, dz, dc) != (0, 0, 0, 0):
                        greeted += 1
                        pl.semaphore_signal(
                            barrier, inc=1,
                            device_id=device((x + dx) % SIDE, (y + dy) % SIDE, (z + dz) % SIDE,
                                             (core + dc) % 2),
                            device_id_type=MESH)

    def weight_copy(which, m):
        cols = pl.ds(m * 2 * n, 2 * n)
        source = (wg.at[:, cols, :], wu.at[:, cols, :], wd.at[:, :, cols])[which]
        return pltpu.make_async_copy(source, (Wg, Wu, Wd)[which].at[m], w_sem.at[which, m])

    def own_tokens(c):
        return pltpu.make_async_copy(tok.at[:, pl.ds(c * n, n)], T.at[c, x], loc.at[c])

    def own_tokens_other(p, r):
        c = r * 4 + KINDS.index(p)
        return pltpu.make_async_copy(
            tok.at[:, pl.ds(c * n, n)], TO.at[p - 1, r, at[p]], loco.at[p - 1, r])

    def small(which):
        source = (sgu, sd, gv)[which]
        return pltpu.make_async_copy(source, (Sg, Sd, Gv)[which], small_sem.at[which])

    def own_meta(which, p):
        source, target = ((ids_in, idv), (mix_in, mixv))[which]
        return pltpu.make_async_copy(
            source, target.at[p, at[p]], small_sem.at[3 + which * 3 + p])

    for p in range(3):
        own_meta(0, p).start()
        own_meta(1, p).start()
    for c in range(chunks):
        own_tokens(c).start()
    for r in range(rounds):
        own_tokens_other(1, r).start()
        own_tokens_other(2, r).start()
    for which in range(3):
        small(which).start()

    pl.semaphore_wait(barrier, greeted)

    def meta_copy(which, p, k):
        source, target = ((ids_in, idv), (mix_in, mixv))[which]
        return pltpu.make_async_remote_copy(
            source, target.at[p, at[p]], m_send.at[which, p, k - 1], m_recv.at[which, p, k - 1],
            device_id=near(p, k)[1], device_id_type=MESH)

    def token_copy(c, k):
        return pltpu.make_async_remote_copy(
            tok.at[:, pl.ds(c * n, n)], T.at[c, x], t_send.at[c, k - 1], t_recv.at[c, k - 1],
            device_id=near(0, k)[1], device_id_type=MESH)

    def token_copy_other(p, r, k):
        c = r * 4 + KINDS.index(p)
        return pltpu.make_async_remote_copy(
            tok.at[:, pl.ds(c * n, n)], TO.at[p - 1, r, at[p]],
            to_send.at[p - 1, r, k - 1], to_recv.at[p - 1, r, k - 1],
            device_id=near(p, k)[1], device_id_type=MESH)

    for p in range(3):
        for k in range(1, SIDE):
            meta_copy(0, p, k).start()
            meta_copy(1, p, k).start()
    for r in range(rounds):
        for q, p in enumerate(KINDS):
            for k in range(1, SIDE):
                if p == 0:
                    token_copy(r * 4 + q, k).start()
                else:
                    token_copy_other(p, r, k).start()
    for m in range(pairs):
        for which in range(3):
            weight_copy(which, m).start()

    def meta_here(which, p):
        own_meta(which, p).wait()
        for k in range(1, SIDE):
            meta_copy(which, p, k).wait_recv()

    def table_for(p):
        meta_here(0, p)
        pick_table(p)

    pair = lax.broadcasted_iota(jnp.int32, (2 * GROUP, rows), 0)
    before = (
        lax.broadcasted_iota(jnp.int32, (rows, rows), 0)
        < lax.broadcasted_iota(jnp.int32, (rows, rows), 1)
    ).astype(F32).astype(BF16)
    rho = lax.broadcasted_iota(jnp.int32, (slots, 2 * GROUP), 0)
    col = lax.broadcasted_iota(jnp.int32, (slots, 2 * GROUP), 1)
    half = ((lax.broadcasted_iota(jnp.int32, (slots, lanes), 0) % 8) // 4).astype(F32)

    mine = (lax.broadcasted_iota(jnp.int32, (slots, lanes), 0) % 4) == (
        lax.broadcasted_iota(jnp.int32, (slots, lanes), 1) // rows)

    def slot_tables(p, weighted):
        by_first = jnp.where(p == 2, 2, 64)
        by_second = jnp.where(p == 1, 2, 16)
        base = jnp.where(p == 0, 2 * x, jnp.where(p == 1, 16 * y, 64 * z))
        expert = (
            base + (pair // 16) * by_first + ((pair // 4) % 4) * by_second
            + ((pair // 2) % 2) * 8 + pair % 2)
        spots, weights = [], []
        for s in range(SIDE):
            chosen = jnp.zeros((2 * GROUP, rows), F32)
            weight = jnp.zeros((2 * GROUP, rows), F32)
            for k in range(top):
                hit = jnp.broadcast_to(idv[p, s, k:k + 1, :], (2 * GROUP, rows)) == expert
                chosen = jnp.where(hit, 1.0, chosen)
                if weighted:
                    mix = mixv[p, s, k:k + 1, :].astype(F32) * (1.0 / 256.0)
                    weight = jnp.where(hit, jnp.broadcast_to(mix, (2 * GROUP, rows)), weight)
            rank = jnp.dot(chosen.astype(BF16), before, preferred_element_type=F32)
            spots.append(jnp.where(chosen > 0.5, rank + 1.0, 0.0).astype(BF16))
            weights.append(weight.astype(BF16))
        spot = jnp.concatenate(spots, axis=1)
        weight = jnp.concatenate(weights, axis=1)
        pos, mixes = [], []
        for e in range(2):
            spread = (col == (rho // 8) * 2 + e).astype(F32).astype(BF16)
            found = jnp.dot(spread, spot, preferred_element_type=F32)
            pos.append(jnp.where(mine & (found > 0.5), found - half, -9.0))
            if weighted:
                mixes.append(jnp.dot(spread, weight, preferred_element_type=F32))
        return pos, mixes

    def pick_table(p):
        pos, _ = slot_tables(p, False)
        for g in range(CAP):
            hot = jnp.where(
                (pos[0] == 2.0 * g + 1.0) | (pos[1] == 2.0 * g - 6.0), 1.0, 0.0).astype(BF16)
            for q in range(lanes // 128):
                D[p, g * (lanes // 128) + q] = hot[:, q * 128:(q + 1) * 128]

    def block_copy(p, c, step, h):
        spot, to = far_peer(p, step)
        span = pl.ds(*OUTWARD[h])
        return pltpu.make_async_remote_copy(
            O.at[c, span, spot], X.at[c, span, place(p)], d_send.at[h, c], d_recv.at[h, c],
            device_id=to, device_id_type=MESH)

    def own_block(p, c, h):
        span = pl.ds(*OUTWARD[h])
        return pltpu.make_async_copy(
            O.at[c, span, place(p)], X.at[c, span, place(p)], own_sem.at[h, c])

    def send_blocks(p, c, h):
        for step in steps:
            block_copy(p, c, step, h).start()
        own_block(p, c, h).start()

    def send_rows(r, q):
        p, c = KINDS[q], r * 4 + q
        if p == 0:
            own_tokens(c).wait()
            for k in range(1, SIDE):
                token_copy(c, k).wait_recv()
            tokens = T[c].reshape(lanes, n)
        else:
            own_tokens_other(p, r).wait()
            for k in range(1, SIDE):
                token_copy_other(p, r, k).wait_recv()
            tokens = TO[p - 1, r].reshape(lanes, n)
        cut = lanes // 128
        picks = jnp.concatenate(
            [jnp.concatenate([D[p, g * cut + b] for b in range(cut)], axis=1)
             for g in range(CAP)], axis=0)
        O[c] = jnp.dot(picks, tokens, preferred_element_type=F32).reshape(
            CAP, GROUP, 8, n).astype(BF16)
        send_blocks(p, c, 0)

    def dispatch(r, carry):
        for q in range(4):
            send_rows(r, q)
        return carry

    for q in (0, 1, 3, 2):
        if q < 2 or q == 3:
            table_for(KINDS[q])
        send_rows(0, q)
    lax.fori_loop(1, rounds, dispatch, 0)

    def second_half(r, carry):
        for q, p in enumerate(KINDS):
            send_blocks(p, r * 4 + q, 1)
        return carry

    lax.fori_loop(0, rounds, second_half, 0)
    for r in range(rounds):
        for q, p in enumerate(KINDS):
            if p != 0:
                for k in range(1, SIDE):
                    token_copy(r * 4 + q, k).start()

    for p in range(3):
        meta_here(1, p)

    def sum_table(p, carry):
        pos, mixes = slot_tables(p, True)
        pos_t, mix_t = [v.T for v in pos], [v.T for v in mixes]
        for g in range(CAP):
            block = (jnp.where(pos_t[0] == 2.0 * g + 1.0, mix_t[0], 0.0)
                     + jnp.where(pos_t[1] == 2.0 * g - 6.0, mix_t[1], 0.0)).astype(BF16)
            for b in range(2):
                D[p, pl.ds((2 * g + b) * 2, 2)] = block[:, b * 128:(b + 1) * 128].reshape(
                    2, lanes // 2, 128)
        return carry

    lax.fori_loop(0, 3, sum_table, 0)

    here = lax.broadcasted_iota(jnp.int32, (slots, slots), 0)
    there = lax.broadcasted_iota(jnp.int32, (slots, slots), 1)

    def reorder(p):
        scale = 16 if p == 1 else 64
        low, high = there % 4, (there // scale) % 4
        moved = there + (high - low) + (low - high) * scale
        return (here == moved).astype(F32).astype(BF16)

    def all_but_own(buf, part, sem):
        view = buf.at[pl.ds(*part), pl.ds(0, GROUP - 1)]
        return pltpu.make_async_copy(view, view, sem)

    def back_copy(p, c, step, h):
        spot, to = far_peer(p, step)
        span = pl.ds(*HOMEWARD[h])
        return pltpu.make_async_remote_copy(
            X.at[c, span, spot], Y.at[c, span, place(p)], y_send.at[h, c], y_recv.at[h, c],
            device_id=to, device_id_type=MESH)

    def own_back(p, c, h):
        span = pl.ds(*HOMEWARD[h])
        return pltpu.make_async_copy(
            X.at[c, span, place(p)], Y.at[c, span, place(p)], yown_sem.at[h, c])

    def send_back(p, c, h):
        for step in steps:
            back_copy(p, c, step, h).start()
        own_back(p, c, h).start()

    upper = (lax.broadcasted_iota(jnp.int32, (slots, ff), 0) % 8) // 4

    for e in range(2):
        acc[...] = jnp.zeros_like(acc)

        def up_step(r, carry):
            for b in range(2):
                m = 2 * r + b
                if e == 0:
                    weight_copy(0, m).wait()
                    weight_copy(1, m).wait()
                for q in (2 * b, 2 * b + 1):
                    own_block(KINDS[q], r * 4 + q, e).wait()
                    all_but_own(X.at[r * 4 + q], OUTWARD[e], d_recv.at[e, r * 4 + q]).wait()
                p = KINDS[2 * b + 1]
                c = r * 4 + 2 * b
                mixed = jnp.concatenate(
                    [X[c + 1, 3 * e + g].reshape(slots, n) for g in range(4)], axis=1)
                mixed = jnp.dot(reorder(p), mixed, preferred_element_type=F32).astype(BF16)
                v = jnp.concatenate(
                    [jnp.concatenate(
                        [X[c, 3 * e + g].reshape(slots, n), mixed[:, g * n:(g + 1) * n]], axis=1)
                     for g in range(4)], axis=0)
                acc[:, :ff] += jnp.dot(v, Wg[m, e], preferred_element_type=F32)
                acc[:, ff:] += jnp.dot(v, Wu[m, e], preferred_element_type=F32)
            return carry

        lax.fori_loop(0, rounds, up_step, 0)

        def hidden(g, carry):
            part = pl.ds(pl.multiple_of(g * slots, slots), slots)
            h = silu_product(acc[part, :ff], acc[part, ff:])
            mixed_row = (g == 3 * (1 - e)).astype(jnp.int32)
            keep = mixed_row * (upper - e) * (1 - 2 * e) <= 0
            H[e, part, :] = jnp.where(keep, h, 0.0).astype(BF16)
            return carry

        lax.fori_loop(0, 4, hidden, 0)

        def down_step(r, carry):
            for b in range(2):
                m = 2 * r + b
                c = r * 4 + 2 * b
                if e == 0:
                    weight_copy(2, m).wait()
                    low = jnp.dot(H[0, :3 * slots], Wd[m, 0], preferred_element_type=F32)
                    made = [low[g * slots:(g + 1) * slots] for g in range(3)]
                else:
                    high = jnp.dot(H[1], Wd[m, 1], preferred_element_type=F32)
                    low = jnp.dot(H[0, 3 * slots:], Wd[m, 0], preferred_element_type=F32)
                    made = [low + high[:slots]]
                    made += [high[g * slots:(g + 1) * slots] for g in range(1, 4)]
                first = HOMEWARD[e][0]
                for g, v in enumerate(made):
                    X[c, first + g] = v[:, :n].reshape(GROUP, 8, n).astype(BF16)
                send_back(0, c, e)
                p = KINDS[2 * b + 1]
                mixed = jnp.concatenate([v[:, n:].astype(BF16) for v in made], axis=1)
                mixed = jnp.dot(reorder(p), mixed, preferred_element_type=F32)
                for g in range(len(made)):
                    X[c + 1, first + g] = mixed[:, g * n:(g + 1) * n].reshape(
                        GROUP, 8, n).astype(BF16)
                send_back(p, c + 1, e)
            return carry

        lax.fori_loop(0, rounds, down_step, 0)

    for which in range(3):
        small(which).wait()
    for r in range(rounds):
        for q, p in enumerate(KINDS):
            if p != 0:
                own_tokens(r * 4 + q).wait()
                for k in range(1, SIDE):
                    token_copy(r * 4 + q, k).wait_recv()
    shared[...] = jnp.zeros_like(shared)

    def shared_step(c, carry):
        tokens = T[c].reshape(lanes, n)
        span = pl.ds(pl.multiple_of(c * n, n), n)
        shared[0] += jnp.dot(tokens, Sg[0, span, :], preferred_element_type=F32)
        shared[1] += jnp.dot(tokens, Sg[1, span, :], preferred_element_type=F32)
        scored = tokens.astype(F32) * Gv[:, span].astype(F32)
        for q in range(n // 128):
            shared[2] += scored[:, q * 128:(q + 1) * 128]
        return carry

    lax.fori_loop(0, chunks, shared_step, 0)
    shared_hidden = silu_product(shared[0], shared[1]).astype(BF16)
    score = jnp.broadcast_to(jnp.sum(shared[2], axis=1, keepdims=True), (lanes, 128))
    shared[2] = 1.0 / (1.0 + jnp.exp(-score))

    def shared_part(c):
        span = pl.ds(pl.multiple_of(c * n, n), n)
        scale = jnp.concatenate([shared[2]] * (n // 128), axis=1)
        return scale * jnp.dot(shared_hidden, Sd[:, span], preferred_element_type=F32)

    tall = rows // 8

    def spot_of(c, which, s):
        return O.at[c, 2 * which + s // 2, pl.ds(pl.multiple_of((s % 2) * tall, tall), tall)]

    def taken(ref):
        return ref[...].astype(F32).reshape(rows, n)

    def sum_copy(p, c, k):
        other, to = near(p, k)
        return pltpu.make_async_remote_copy(
            spot_of(c, 0, other), rs_in.at[c, at[p]], r_send.at[c, k - 1], r_recv.at[c, k - 1],
            device_id=to, device_id_type=MESH)

    def shared_copy(m, k):
        other, to = near(0, k)
        return pltpu.make_async_remote_copy(
            spot_of(2 * m + 1, 1, other), sh_in.at[m, x], s_send.at[m, k - 1], s_recv.at[m, k - 1],
            device_id=to, device_id_type=MESH)

    def sent(c, carry):
        for h in range(2):
            all_but_own(O.at[c], OUTWARD[h], d_send.at[h, c]).wait()
        return carry

    lax.fori_loop(0, chunks, sent, 0)

    def shared_sums(m, carry):
        O[2 * m + 1, 2:4] = shared_part(2 * m + 1).reshape(2, GROUP, 8, n).astype(BF16)
        for k in range(1, SIDE):
            shared_copy(m, k).start()
        return carry

    lax.fori_loop(0, pairs, shared_sums, 0)

    def finish(r, carry):
        for q, p in enumerate(KINDS):
            c = r * 4 + q
            for k in range(1, SIDE):
                sum_copy(p, c, k).wait_recv()
            total = taken(spot_of(c, 0, at[p]))
            for k in range(1, SIDE):
                total = total + taken(rs_in.at[c, near(p, k)[0]])
            if p != 0:
                m = c // 2
                for k in range(1, SIDE):
                    shared_copy(m, k).wait_recv()
                total = total + taken(spot_of(c, 1, x))
                for k in range(1, SIDE):
                    total = total + taken(sh_in.at[m, near(0, k)[0]])
            out[:, pl.ds(pl.multiple_of(c * n, n), n)] = total.astype(BF16)
        return carry

    def combine(r, carry):
        for q, p in enumerate(KINDS):
            c = r * 4 + q
            for h in range(2):
                own_back(p, c, h).wait()
                all_but_own(Y.at[c], HOMEWARD[h], y_recv.at[h, c]).wait()
            table = jnp.concatenate(
                [D[p, 2 * b:2 * b + 2].reshape(lanes, 128) for b in range(2 * CAP)], axis=1)
            part = jnp.dot(
                table, Y[c].reshape(CAP * slots, n), preferred_element_type=F32)
            if p == 0:
                part = part + shared_part(c)
            O[c, 0:2] = part.reshape(2, GROUP, 8, n).astype(BF16)
            for k in range(1, SIDE):
                sum_copy(p, c, k).start()
        return carry

    lax.fori_loop(0, rounds, combine, 0)

    lax.fori_loop(0, rounds, finish, 0)

    for p in range(3):
        for k in range(1, SIDE):
            meta_copy(0, p, k).wait_send()
            meta_copy(1, p, k).wait_send()

    def drain(r, carry):
        for q, p in enumerate(KINDS):
            c = r * 4 + q
            for k in range(1, SIDE):
                token_copy(c, k).wait_send()
                sum_copy(p, c, k).wait_send()
                if p != 0:
                    token_copy_other(p, r, k).wait_send()
                    shared_copy(c // 2, k).wait_send()
            for h in range(2):
                all_but_own(X.at[c], HOMEWARD[h], y_send.at[h, c]).wait()
        return carry

    lax.fori_loop(0, rounds, drain, 0)


def on_device(chunks, tokens, expert_ids, combine, w_gate, w_up, w_down, gate_up, down, gate_vec):
    rows, model = tokens.shape
    top = expert_ids.shape[1]
    ff, hid = w_gate.shape[2], down.shape[0]
    n = model // chunks
    slots = GROUP * 8
    lanes = SIDE * rows
    rounds, pairs = chunks // 4, chunks // 2
    near = SIDE - 1
    cfg = (chunks, n, rows, model, ff, hid, top)
    any_spec = pl.BlockSpec(memory_space=pl.ANY)
    dma = pltpu.SemaphoreType.DMA
    return pl.pallas_call(
        functools.partial(kernel, cfg),
        out_shape=jax.ShapeDtypeStruct((rows, model), BF16),
        in_specs=[any_spec] * 9,
        out_specs=pl.BlockSpec(memory_space=pltpu.VMEM),
        scratch_shapes=[
            pltpu.VMEM((chunks, SIDE, rows, n), BF16),
            pltpu.VMEM((2, rounds, SIDE, rows, n), BF16),
            pltpu.VMEM((3, SIDE, top, rows), jnp.int32),
            pltpu.VMEM((3, SIDE, top, rows), jnp.int32),
            pltpu.VMEM((3, 4 * CAP, 256, 128), BF16),
            pltpu.VMEM((chunks, CAP, GROUP, 8, n), BF16),
            pltpu.VMEM((chunks, CAP, GROUP, 8, n), BF16),
            pltpu.VMEM((chunks, CAP, GROUP, 8, n), BF16),
            pltpu.VMEM((pairs, 2, 2 * n, ff), BF16),
            pltpu.VMEM((pairs, 2, 2 * n, ff), BF16),
            pltpu.VMEM((pairs, 2, ff, 2 * n), BF16),
            pltpu.VMEM((4 * slots, 2 * ff), F32),
            pltpu.VMEM((2, 4 * slots, ff), BF16),
            pltpu.VMEM((2, model, hid), BF16),
            pltpu.VMEM((hid, model), BF16),
            pltpu.VMEM((1, model), BF16),
            pltpu.VMEM((3, lanes, hid), F32),
            pltpu.VMEM((chunks, SIDE, rows // 8, 8, n), BF16),
            pltpu.VMEM((pairs, SIDE, rows // 8, 8, n), BF16),
            dma((2, 3, near)), dma((2, 3, near)),
            dma((chunks, near)), dma((chunks, near)),
            dma((2, rounds, near)), dma((2, rounds, near)),
            dma((2, chunks)), dma((2, chunks)),
            dma((2, chunks)), dma((2, chunks)),
            dma((chunks, near)), dma((chunks, near)),
            dma((pairs, near)), dma((pairs, near)),
            dma((chunks,)), dma((2, rounds)), dma((3, pairs)),
            dma((2, chunks)), dma((2, chunks)), dma((9,)),
        ],
        compiler_params=pltpu.CompilerParams(
            collective_id=0, has_side_effects=True, vmem_limit_bytes=67043328),
    )(tokens, expert_ids.T, combine.T, w_gate, w_up, w_down, gate_up, down,
      gate_vec.reshape(1, model))


def solution(mesh, chunks=8):
    return jax.shard_map(
        functools.partial(on_device, chunks),
        mesh=mesh,
        in_specs=(
            P(("wide", "narrow"), None),
            P(("wide", "narrow"), None),
            P(("wide", "narrow"), None),
            P(("wide", "narrow"), None, None),
            P(("wide", "narrow"), None, None),
            P(("wide", "narrow"), None, None),
            P(None, None, "narrow"),
            P("narrow", None),
            P(),
        ),
        out_specs=P(("wide", "narrow"), None),
        check_vma=False,
    )
```

```python
import functools

import jax
import jax.numpy as jnp
from jax import lax
from jax.experimental import pallas as pl
from jax.experimental.pallas import tpu as pltpu
from jax.sharding import PartitionSpec as P

CAP = 7
MESH = pl.DeviceIdType.MESH
F32 = jnp.float32
BF16 = jnp.bfloat16


SIDE = 4
GROUP = 2 * SIDE * SIDE
KINDS = (0, 1, 0, 2)
OUTWARD = ((0, 4), (4, 3))
HOMEWARD = ((0, 3), (3, 4))


def offsets():
    steps = [(da, db, dc) for da in range(SIDE) for db in range(SIDE) for dc in range(2)]
    steps = steps[1:]

    def far(step):
        return min(step[0], SIDE - step[0]) + min(step[1], SIDE - step[1])

    ordered = sorted(steps, key=lambda s: (-far(s), (s[0] + 2 * s[1]) % 4, s[2]))
    mixed = []
    while ordered:
        mixed.append(ordered.pop(0))
        if ordered:
            mixed.append(ordered.pop())
    return mixed


def silu_product(gate, up):
    return gate * (1.0 / (1.0 + jnp.exp(-gate))) * up


def kernel(
    cfg,
    tok, ids_in, mix_in, wg, wu, wd, sgu, sd, gv,
    out,
    T, TO, idv, mixv, D, O, X, Y, Wg, Wu, Wd, acc, H, Sg, Sd, Gv, shared, rs_in, sh_in,
    m_send, m_recv, t_send, t_recv, to_send, to_recv, d_send, d_recv, y_send, y_recv,
    r_send, r_recv, s_send, s_recv, loc, loco, w_sem, own_sem, yown_sem, small_sem,
):
    chunks, n, rows, model, ff, hid, top = cfg
    w = lax.axis_index("wide")
    x = lax.axis_index("narrow")
    core, y, z = w % 2, (w // 2) % SIDE, w // (2 * SIDE)
    at = (x, y, z)
    rounds, pairs = chunks // 4, chunks // 2
    lanes = SIDE * rows
    slots = GROUP * 8
    steps = offsets()

    def device(xx, yy, zz, cc):
        return ((zz * SIDE + yy) * 2 + cc, xx)

    def place(p):
        first, second = ((z, y), (z, x), (x, y))[p]
        return (first * SIDE + second) * 2 + core

    def far_peer(p, step):
        da, db, dc = step
        first, second = ((z, y), (z, x), (x, y))[p]
        first, second, cc = (first + da) % SIDE, (second + db) % SIDE, (core + dc) % 2
        spot = ((x, second, first), (second, y, first), (first, second, z))[p]
        return (first * SIDE + second) * 2 + cc, device(*spot, cc)

    def near(p, k):
        other = (at[p] + k) % SIDE
        spot = tuple(other if q == p else at[q] for q in range(3))
        return other, device(*spot, core)

    barrier = pltpu.get_barrier_semaphore()
    greeted = 0
    for dx in range(SIDE):
        for dy in range(SIDE):
            for dz in range(SIDE):
                for dc in range(2):
                    if dx * dy * dz == 0 and (dx, dy, dz, dc) != (0, 0, 0, 0):
                        greeted += 1
                        pl.semaphore_signal(
                            barrier, inc=1,
                            device_id=device((x + dx) % SIDE, (y + dy) % SIDE, (z + dz) % SIDE,
                                             (core + dc) % 2),
                            device_id_type=MESH)

    def weight_copy(which, m):
        cols = pl.ds(m * 2 * n, 2 * n)
        source = (wg.at[:, cols, :], wu.at[:, cols, :], wd.at[:, :, cols])[which]
        return pltpu.make_async_copy(source, (Wg, Wu, Wd)[which].at[m], w_sem.at[which, m])

    def own_tokens(c):
        return pltpu.make_async_copy(tok.at[:, pl.ds(c * n, n)], T.at[c, x], loc.at[c])

    def own_tokens_other(p, r):
        c = r * 4 + KINDS.index(p)
        return pltpu.make_async_copy(
            tok.at[:, pl.ds(c * n, n)], TO.at[p - 1, r, at[p]], loco.at[p - 1, r])

    def small(which):
        source = (sgu, sd, gv)[which]
        return pltpu.make_async_copy(source, (Sg, Sd, Gv)[which], small_sem.at[which])

    def own_meta(which, p):
        source, target = ((ids_in, idv), (mix_in, mixv))[which]
        return pltpu.make_async_copy(
            source, target.at[p, at[p]], small_sem.at[3 + which * 3 + p])

    for p in range(3):
        own_meta(0, p).start()
        own_meta(1, p).start()
    for c in range(chunks):
        own_tokens(c).start()
    for r in range(rounds):
        own_tokens_other(1, r).start()
        own_tokens_other(2, r).start()
    for which in range(3):
        small(which).start()

    pl.semaphore_wait(barrier, greeted)

    def meta_copy(which, p, k):
        source, target = ((ids_in, idv), (mix_in, mixv))[which]
        return pltpu.make_async_remote_copy(
            source, target.at[p, at[p]], m_send.at[which, p, k - 1], m_recv.at[which, p, k - 1],
            device_id=near(p, k)[1], device_id_type=MESH)

    def token_copy(c, k):
        return pltpu.make_async_remote_copy(
            tok.at[:, pl.ds(c * n, n)], T.at[c, x], t_send.at[c, k - 1], t_recv.at[c, k - 1],
            device_id=near(0, k)[1], device_id_type=MESH)

    def token_copy_other(p, r, k):
        c = r * 4 + KINDS.index(p)
        return pltpu.make_async_remote_copy(
            tok.at[:, pl.ds(c * n, n)], TO.at[p - 1, r, at[p]],
            to_send.at[p - 1, r, k - 1], to_recv.at[p - 1, r, k - 1],
            device_id=near(p, k)[1], device_id_type=MESH)

    for p in range(3):
        for k in range(1, SIDE):
            meta_copy(0, p, k).start()
            meta_copy(1, p, k).start()
    for r in range(rounds):
        for q, p in enumerate(KINDS):
            for k in range(1, SIDE):
                if p == 0:
                    token_copy(r * 4 + q, k).start()
                else:
                    token_copy_other(p, r, k).start()
    for m in range(pairs):
        for which in range(3):
            weight_copy(which, m).start()

    def meta_here(which, p):
        own_meta(which, p).wait()
        for k in range(1, SIDE):
            meta_copy(which, p, k).wait_recv()

    def table_for(p):
        meta_here(0, p)
        pick_table(p)

    pair = lax.broadcasted_iota(jnp.int32, (2 * GROUP, rows), 0)
    before = (
        lax.broadcasted_iota(jnp.int32, (rows, rows), 0)
        < lax.broadcasted_iota(jnp.int32, (rows, rows), 1)
    ).astype(F32).astype(BF16)
    rho = lax.broadcasted_iota(jnp.int32, (slots, 2 * GROUP), 0)
    col = lax.broadcasted_iota(jnp.int32, (slots, 2 * GROUP), 1)
    half = ((lax.broadcasted_iota(jnp.int32, (slots, lanes), 0) % 8) // 4).astype(F32)

    mine = (lax.broadcasted_iota(jnp.int32, (slots, lanes), 0) % 4) == (
        lax.broadcasted_iota(jnp.int32, (slots, lanes), 1) // rows)

    def slot_tables(p, weighted):
        by_first = jnp.where(p == 2, 2, 64)
        by_second = jnp.where(p == 1, 2, 16)
        base = jnp.where(p == 0, 2 * x, jnp.where(p == 1, 16 * y, 64 * z))
        expert = (
            base + (pair // 16) * by_first + ((pair // 4) % 4) * by_second
            + ((pair // 2) % 2) * 8 + pair % 2)
        spots, weights = [], []
        for s in range(SIDE):
            chosen = jnp.zeros((2 * GROUP, rows), F32)
            weight = jnp.zeros((2 * GROUP, rows), F32)
            for k in range(top):
                hit = jnp.broadcast_to(idv[p, s, k:k + 1, :], (2 * GROUP, rows)) == expert
                chosen = jnp.where(hit, 1.0, chosen)
                if weighted:
                    mix = mixv[p, s, k:k + 1, :].astype(F32) * (1.0 / 256.0)
                    weight = jnp.where(hit, jnp.broadcast_to(mix, (2 * GROUP, rows)), weight)
            rank = jnp.dot(chosen.astype(BF16), before, preferred_element_type=F32)
            spots.append(jnp.where(chosen > 0.5, rank + 1.0, 0.0).astype(BF16))
            weights.append(weight.astype(BF16))
        spot = jnp.concatenate(spots, axis=1)
        weight = jnp.concatenate(weights, axis=1)
        pos, mixes = [], []
        for e in range(2):
            spread = (col == (rho // 8) * 2 + e).astype(F32).astype(BF16)
            found = jnp.dot(spread, spot, preferred_element_type=F32)
            pos.append(jnp.where(mine & (found > 0.5), found - half, -9.0))
            if weighted:
                mixes.append(jnp.dot(spread, weight, preferred_element_type=F32))
        return pos, mixes

    def pick_table(p):
        pos, _ = slot_tables(p, False)
        for g in range(CAP):
            hot = jnp.where(
                (pos[0] == 2.0 * g + 1.0) | (pos[1] == 2.0 * g - 6.0), 1.0, 0.0).astype(BF16)
            for q in range(lanes // 128):
                D[p, g * (lanes // 128) + q] = hot[:, q * 128:(q + 1) * 128]

    def block_copy(p, c, step, h):
        spot, to = far_peer(p, step)
        span = pl.ds(*OUTWARD[h])
        return pltpu.make_async_remote_copy(
            O.at[c, span, spot], X.at[c, span, place(p)], d_send.at[h, c], d_recv.at[h, c],
            device_id=to, device_id_type=MESH)

    def own_block(p, c, h):
        span = pl.ds(*OUTWARD[h])
        return pltpu.make_async_copy(
            O.at[c, span, place(p)], X.at[c, span, place(p)], own_sem.at[h, c])

    def send_blocks(p, c, h):
        for step in steps:
            block_copy(p, c, step, h).start()
        own_block(p, c, h).start()

    def send_rows(r, q):
        p, c = KINDS[q], r * 4 + q
        if p == 0:
            own_tokens(c).wait()
            for k in range(1, SIDE):
                token_copy(c, k).wait_recv()
            tokens = T[c].reshape(lanes, n)
        else:
            own_tokens_other(p, r).wait()
            for k in range(1, SIDE):
                token_copy_other(p, r, k).wait_recv()
            tokens = TO[p - 1, r].reshape(lanes, n)
        cut = lanes // 128
        picks = jnp.concatenate(
            [jnp.concatenate([D[p, g * cut + b] for b in range(cut)], axis=1)
             for g in range(CAP)], axis=0)
        O[c] = jnp.dot(picks, tokens, preferred_element_type=F32).reshape(
            CAP, GROUP, 8, n).astype(BF16)
        send_blocks(p, c, 0)

    def dispatch(r, carry):
        for q in range(4):
            send_rows(r, q)
        return carry

    for q in (0, 1, 3, 2):
        if q < 2 or q == 3:
            table_for(KINDS[q])
        send_rows(0, q)
    lax.fori_loop(1, rounds, dispatch, 0)

    def second_half(r, carry):
        for q, p in enumerate(KINDS):
            send_blocks(p, r * 4 + q, 1)
        return carry

    lax.fori_loop(0, rounds, second_half, 0)
    for r in range(rounds):
        for q, p in enumerate(KINDS):
            if p != 0:
                for k in range(1, SIDE):
                    token_copy(r * 4 + q, k).start()

    for p in range(3):
        meta_here(1, p)

    def sum_table(p, carry):
        pos, mixes = slot_tables(p, True)
        pos_t, mix_t = [v.T for v in pos], [v.T for v in mixes]
        for g in range(CAP):
            block = (jnp.where(pos_t[0] == 2.0 * g + 1.0, mix_t[0], 0.0)
                     + jnp.where(pos_t[1] == 2.0 * g - 6.0, mix_t[1], 0.0)).astype(BF16)
            for b in range(2):
                D[p, pl.ds((2 * g + b) * 2, 2)] = block[:, b * 128:(b + 1) * 128].reshape(
                    2, lanes // 2, 128)
        return carry

    lax.fori_loop(0, 3, sum_table, 0)

    here = lax.broadcasted_iota(jnp.int32, (slots, slots), 0)
    there = lax.broadcasted_iota(jnp.int32, (slots, slots), 1)

    def reorder(p):
        scale = 16 if p == 1 else 64
        low, high = there % 4, (there // scale) % 4
        moved = there + (high - low) + (low - high) * scale
        return (here == moved).astype(F32).astype(BF16)

    def all_but_own(buf, part, sem):
        view = buf.at[pl.ds(*part), pl.ds(0, GROUP - 1)]
        return pltpu.make_async_copy(view, view, sem)

    def back_copy(p, c, step, h):
        spot, to = far_peer(p, step)
        span = pl.ds(*HOMEWARD[h])
        return pltpu.make_async_remote_copy(
            X.at[c, span, spot], Y.at[c, span, place(p)], y_send.at[h, c], y_recv.at[h, c],
            device_id=to, device_id_type=MESH)

    def own_back(p, c, h):
        span = pl.ds(*HOMEWARD[h])
        return pltpu.make_async_copy(
            X.at[c, span, place(p)], Y.at[c, span, place(p)], yown_sem.at[h, c])

    def send_back(p, c, h):
        for step in steps:
            back_copy(p, c, step, h).start()
        own_back(p, c, h).start()

    upper = (lax.broadcasted_iota(jnp.int32, (slots, ff), 0) % 8) // 4

    for e in range(2):
        acc[...] = jnp.zeros_like(acc)

        def up_step(r, carry):
            for b in range(2):
                m = 2 * r + b
                if e == 0:
                    weight_copy(0, m).wait()
                    weight_copy(1, m).wait()
                for q in (2 * b, 2 * b + 1):
                    own_block(KINDS[q], r * 4 + q, e).wait()
                    all_but_own(X.at[r * 4 + q], OUTWARD[e], d_recv.at[e, r * 4 + q]).wait()
                p = KINDS[2 * b + 1]
                c = r * 4 + 2 * b
                mixed = jnp.concatenate(
                    [X[c + 1, 3 * e + g].reshape(slots, n) for g in range(4)], axis=1)
                mixed = jnp.dot(reorder(p), mixed, preferred_element_type=F32).astype(BF16)
                v = jnp.concatenate(
                    [jnp.concatenate(
                        [X[c, 3 * e + g].reshape(slots, n), mixed[:, g * n:(g + 1) * n]], axis=1)
                     for g in range(4)], axis=0)
                acc[:, :ff] += jnp.dot(v, Wg[m, e], preferred_element_type=F32)
                acc[:, ff:] += jnp.dot(v, Wu[m, e], preferred_element_type=F32)
            return carry

        lax.fori_loop(0, rounds, up_step, 0)

        def hidden(g, carry):
            part = pl.ds(pl.multiple_of(g * slots, slots), slots)
            h = silu_product(acc[part, :ff], acc[part, ff:])
            mixed_row = (g == 3 * (1 - e)).astype(jnp.int32)
            keep = mixed_row * (upper - e) * (1 - 2 * e) <= 0
            H[e, part, :] = jnp.where(keep, h, 0.0).astype(BF16)
            return carry

        lax.fori_loop(0, 4, hidden, 0)

        def down_step(r, carry):
            for b in range(2):
                m = 2 * r + b
                c = r * 4 + 2 * b
                if e == 0:
                    weight_copy(2, m).wait()
                    low = jnp.dot(H[0, :3 * slots], Wd[m, 0], preferred_element_type=F32)
                    made = [low[g * slots:(g + 1) * slots] for g in range(3)]
                else:
                    high = jnp.dot(H[1], Wd[m, 1], preferred_element_type=F32)
                    low = jnp.dot(H[0, 3 * slots:], Wd[m, 0], preferred_element_type=F32)
                    made = [low + high[:slots]]
                    made += [high[g * slots:(g + 1) * slots] for g in range(1, 4)]
                first = HOMEWARD[e][0]
                for g, v in enumerate(made):
                    X[c, first + g] = v[:, :n].reshape(GROUP, 8, n).astype(BF16)
                send_back(0, c, e)
                p = KINDS[2 * b + 1]
                mixed = jnp.concatenate([v[:, n:].astype(BF16) for v in made], axis=1)
                mixed = jnp.dot(reorder(p), mixed, preferred_element_type=F32)
                for g in range(len(made)):
                    X[c + 1, first + g] = mixed[:, g * n:(g + 1) * n].reshape(
                        GROUP, 8, n).astype(BF16)
                send_back(p, c + 1, e)
            return carry

        lax.fori_loop(0, rounds, down_step, 0)

    for which in range(3):
        small(which).wait()
    for r in range(rounds):
        for q, p in enumerate(KINDS):
            if p != 0:
                own_tokens(r * 4 + q).wait()
                for k in range(1, SIDE):
                    token_copy(r * 4 + q, k).wait_recv()
    shared[...] = jnp.zeros_like(shared)

    def shared_step(c, carry):
        tokens = T[c].reshape(lanes, n)
        span = pl.ds(pl.multiple_of(c * n, n), n)
        shared[0] += jnp.dot(tokens, Sg[0, span, :], preferred_element_type=F32)
        shared[1] += jnp.dot(tokens, Sg[1, span, :], preferred_element_type=F32)
        scored = tokens.astype(F32) * Gv[:, span].astype(F32)
        for q in range(n // 128):
            shared[2] += scored[:, q * 128:(q + 1) * 128]
        return carry

    lax.fori_loop(0, chunks, shared_step, 0)
    shared_hidden = silu_product(shared[0], shared[1]).astype(BF16)
    score = jnp.broadcast_to(jnp.sum(shared[2], axis=1, keepdims=True), (lanes, 128))
    shared[2] = 1.0 / (1.0 + jnp.exp(-score))

    def shared_part(c):
        span = pl.ds(pl.multiple_of(c * n, n), n)
        scale = jnp.concatenate([shared[2]] * (n // 128), axis=1)
        return scale * jnp.dot(shared_hidden, Sd[:, span], preferred_element_type=F32)

    tall = rows // 8

    def spot_of(c, which, s):
        return O.at[c, 2 * which + s // 2, pl.ds(pl.multiple_of((s % 2) * tall, tall), tall)]

    def taken(ref):
        return ref[...].astype(F32).reshape(rows, n)

    def sum_copy(p, c, k):
        other, to = near(p, k)
        return pltpu.make_async_remote_copy(
            spot_of(c, 0, other), rs_in.at[c, at[p]], r_send.at[c, k - 1], r_recv.at[c, k - 1],
            device_id=to, device_id_type=MESH)

    def shared_copy(m, k):
        other, to = near(0, k)
        return pltpu.make_async_remote_copy(
            spot_of(2 * m + 1, 1, other), sh_in.at[m, x], s_send.at[m, k - 1], s_recv.at[m, k - 1],
            device_id=to, device_id_type=MESH)

    def sent(c, carry):
        for h in range(2):
            all_but_own(O.at[c], OUTWARD[h], d_send.at[h, c]).wait()
        return carry

    lax.fori_loop(0, chunks, sent, 0)

    def shared_sums(m, carry):
        O[2 * m + 1, 2:4] = shared_part(2 * m + 1).reshape(2, GROUP, 8, n).astype(BF16)
        for k in range(1, SIDE):
            shared_copy(m, k).start()
        return carry

    lax.fori_loop(0, pairs, shared_sums, 0)

    def finish(r, carry):
        for q, p in enumerate(KINDS):
            c = r * 4 + q
            for k in range(1, SIDE):
                sum_copy(p, c, k).wait_recv()
            total = taken(spot_of(c, 0, at[p]))
            for k in range(1, SIDE):
                total = total + taken(rs_in.at[c, near(p, k)[0]])
            if p != 0:
                m = c // 2
                for k in range(1, SIDE):
                    shared_copy(m, k).wait_recv()
                total = total + taken(spot_of(c, 1, x))
                for k in range(1, SIDE):
                    total = total + taken(sh_in.at[m, near(0, k)[0]])
            out[:, pl.ds(pl.multiple_of(c * n, n), n)] = total.astype(BF16)
        return carry

    def combine(r, carry):
        for q, p in enumerate(KINDS):
            c = r * 4 + q
            for h in range(2):
                own_back(p, c, h).wait()
                all_but_own(Y.at[c], HOMEWARD[h], y_recv.at[h, c]).wait()
            table = jnp.concatenate(
                [D[p, 2 * b:2 * b + 2].reshape(lanes, 128) for b in range(2 * CAP)], axis=1)
            part = jnp.dot(
                table, Y[c].reshape(CAP * slots, n), preferred_element_type=F32)
            if p == 0:
                part = part + shared_part(c)
            O[c, 0:2] = part.reshape(2, GROUP, 8, n).astype(BF16)
            for k in range(1, SIDE):
                sum_copy(p, c, k).start()
        return carry

    lax.fori_loop(0, rounds, combine, 0)

    lax.fori_loop(0, rounds, finish, 0)

    for p in range(3):
        for k in range(1, SIDE):
            meta_copy(0, p, k).wait_send()
            meta_copy(1, p, k).wait_send()

    def drain(r, carry):
        for q, p in enumerate(KINDS):
            c = r * 4 + q
            for k in range(1, SIDE):
                token_copy(c, k).wait_send()
                sum_copy(p, c, k).wait_send()
                if p != 0:
                    token_copy_other(p, r, k).wait_send()
                    shared_copy(c // 2, k).wait_send()
            for h in range(2):
                all_but_own(X.at[c], HOMEWARD[h], y_send.at[h, c]).wait()
        return carry

    lax.fori_loop(0, rounds, drain, 0)


def on_device(chunks, tokens, expert_ids, combine, w_gate, w_up, w_down, gate_up, down, gate_vec):
    rows, model = tokens.shape
    top = expert_ids.shape[1]
    ff, hid = w_gate.shape[2], down.shape[0]
    n = model // chunks
    slots = GROUP * 8
    lanes = SIDE * rows
    rounds, pairs = chunks // 4, chunks // 2
    near = SIDE - 1
    cfg = (chunks, n, rows, model, ff, hid, top)
    any_spec = pl.BlockSpec(memory_space=pl.ANY)
    dma = pltpu.SemaphoreType.DMA
    return pl.pallas_call(
        functools.partial(kernel, cfg),
        out_shape=jax.ShapeDtypeStruct((rows, model), BF16),
        in_specs=[any_spec] * 9,
        out_specs=pl.BlockSpec(memory_space=pltpu.VMEM),
        scratch_shapes=[
            pltpu.VMEM((chunks, SIDE, rows, n), BF16),
            pltpu.VMEM((2, rounds, SIDE, rows, n), BF16),
            pltpu.VMEM((3, SIDE, top, rows), jnp.int32),
            pltpu.VMEM((3, SIDE, top, rows), jnp.int32),
            pltpu.VMEM((3, 4 * CAP, 256, 128), BF16),
            pltpu.VMEM((chunks, CAP, GROUP, 8, n), BF16),
            pltpu.VMEM((chunks, CAP, GROUP, 8, n), BF16),
            pltpu.VMEM((chunks, CAP, GROUP, 8, n), BF16),
            pltpu.VMEM((pairs, 2, 2 * n, ff), BF16),
            pltpu.VMEM((pairs, 2, 2 * n, ff), BF16),
            pltpu.VMEM((pairs, 2, ff, 2 * n), BF16),
            pltpu.VMEM((4 * slots, 2 * ff), F32),
            pltpu.VMEM((2, 4 * slots, ff), BF16),
            pltpu.VMEM((2, model, hid), BF16),
            pltpu.VMEM((hid, model), BF16),
            pltpu.VMEM((1, model), BF16),
            pltpu.VMEM((3, lanes, hid), F32),
            pltpu.VMEM((chunks, SIDE, rows // 8, 8, n), BF16),
            pltpu.VMEM((pairs, SIDE, rows // 8, 8, n), BF16),
            dma((2, 3, near)), dma((2, 3, near)),
            dma((chunks, near)), dma((chunks, near)),
            dma((2, rounds, near)), dma((2, rounds, near)),
            dma((2, chunks)), dma((2, chunks)),
            dma((2, chunks)), dma((2, chunks)),
            dma((chunks, near)), dma((chunks, near)),
            dma((pairs, near)), dma((pairs, near)),
            dma((chunks,)), dma((2, rounds)), dma((3, pairs)),
            dma((2, chunks)), dma((2, chunks)), dma((9,)),
        ],
        compiler_params=pltpu.CompilerParams(
            collective_id=0, has_side_effects=True, vmem_limit_bytes=67043328),
    )(tokens, expert_ids.T, combine.T, w_gate, w_up, w_down, gate_up, down,
      gate_vec.reshape(1, model))


def solution(mesh, chunks=8):
    return jax.shard_map(
        functools.partial(on_device, chunks),
        mesh=mesh,
        in_specs=(
            P(("wide", "narrow"), None),
            P(("wide", "narrow"), None),
            P(("wide", "narrow"), None),
            P(("wide", "narrow"), None, None),
            P(("wide", "narrow"), None, None),
            P(("wide", "narrow"), None, None),
            P(None, None, "narrow"),
            P("narrow", None),
            P(),
        ),
        out_specs=P(("wide", "narrow"), None),
        check_vma=False,
    )
```

```python
import functools

import jax
import jax.numpy as jnp
from jax import lax
from jax.experimental import pallas as pl
from jax.experimental.pallas import tpu as pltpu
from jax.sharding import PartitionSpec as P

CAP = 7
MESH = pl.DeviceIdType.MESH
F32 = jnp.float32
BF16 = jnp.bfloat16


SIDE = 4
GROUP = 2 * SIDE * SIDE
KINDS = (0, 1, 0, 2)
OUTWARD = ((0, 4), (4, 3))
HOMEWARD = ((0, 3), (3, 4))


def offsets():
    steps = [(da, db, dc) for da in range(SIDE) for db in range(SIDE) for dc in range(2)]
    steps = steps[1:]

    def far(step):
        return min(step[0], SIDE - step[0]) + min(step[1], SIDE - step[1])

    ordered = sorted(steps, key=lambda s: (-far(s), (s[0] + 2 * s[1]) % 4, s[2]))
    mixed = []
    while ordered:
        mixed.append(ordered.pop(0))
        if ordered:
            mixed.append(ordered.pop())
    return mixed


def silu_product(gate, up):
    return gate * (1.0 / (1.0 + jnp.exp(-gate))) * up


def kernel(
    cfg,
    tok, ids_in, mix_in, wg, wu, wd, sgu, sd, gv,
    out,
    T, TO, idv, mixv, D, O, X, Y, Wg, Wu, Wd, acc, H, Sg, Sd, Gv, shared, rs_in, sh_in,
    m_send, m_recv, t_send, t_recv, to_send, to_recv, d_send, d_recv, y_send, y_recv,
    r_send, r_recv, s_send, s_recv, loc, loco, w_sem, own_sem, yown_sem, small_sem,
):
    chunks, n, rows, model, ff, hid, top = cfg
    w = lax.axis_index("wide")
    x = lax.axis_index("narrow")
    core, y, z = w % 2, (w // 2) % SIDE, w // (2 * SIDE)
    at = (x, y, z)
    rounds, pairs = chunks // 4, chunks // 2
    lanes = SIDE * rows
    slots = GROUP * 8
    steps = offsets()

    def device(xx, yy, zz, cc):
        return ((zz * SIDE + yy) * 2 + cc, xx)

    def place(p):
        first, second = ((z, y), (z, x), (x, y))[p]
        return (first * SIDE + second) * 2 + core

    def far_peer(p, step):
        da, db, dc = step
        first, second = ((z, y), (z, x), (x, y))[p]
        first, second, cc = (first + da) % SIDE, (second + db) % SIDE, (core + dc) % 2
        spot = ((x, second, first), (second, y, first), (first, second, z))[p]
        return (first * SIDE + second) * 2 + cc, device(*spot, cc)

    def near(p, k):
        other = (at[p] + k) % SIDE
        spot = tuple(other if q == p else at[q] for q in range(3))
        return other, device(*spot, core)

    barrier = pltpu.get_barrier_semaphore()
    greeted = 0
    for dx in range(SIDE):
        for dy in range(SIDE):
            for dz in range(SIDE):
                for dc in range(2):
                    if dx * dy * dz == 0 and (dx, dy, dz, dc) != (0, 0, 0, 0):
                        greeted += 1
                        pl.semaphore_signal(
                            barrier, inc=1,
                            device_id=device((x + dx) % SIDE, (y + dy) % SIDE, (z + dz) % SIDE,
                                             (core + dc) % 2),
                            device_id_type=MESH)

    def weight_copy(which, m):
        cols = pl.ds(m * 2 * n, 2 * n)
        source = (wg.at[:, cols, :], wu.at[:, cols, :], wd.at[:, :, cols])[which]
        return pltpu.make_async_copy(source, (Wg, Wu, Wd)[which].at[m], w_sem.at[which, m])

    def own_tokens(c):
        return pltpu.make_async_copy(tok.at[:, pl.ds(c * n, n)], T.at[c, x], loc.at[c])

    def own_tokens_other(p, r):
        c = r * 4 + KINDS.index(p)
        return pltpu.make_async_copy(
            tok.at[:, pl.ds(c * n, n)], TO.at[p - 1, r, at[p]], loco.at[p - 1, r])

    def small(which):
        source = (sgu, sd, gv)[which]
        return pltpu.make_async_copy(source, (Sg, Sd, Gv)[which], small_sem.at[which])

    def own_meta(which, p):
        source, target = ((ids_in, idv), (mix_in, mixv))[which]
        return pltpu.make_async_copy(
            source, target.at[p, at[p]], small_sem.at[3 + which * 3 + p])

    for p in range(3):
        own_meta(0, p).start()
        own_meta(1, p).start()
    for c in range(chunks):
        own_tokens(c).start()
    for r in range(rounds):
        own_tokens_other(1, r).start()
        own_tokens_other(2, r).start()
    for which in range(3):
        small(which).start()

    pl.semaphore_wait(barrier, greeted)

    def meta_copy(which, p, k):
        source, target = ((ids_in, idv), (mix_in, mixv))[which]
        return pltpu.make_async_remote_copy(
            source, target.at[p, at[p]], m_send.at[which, p, k - 1], m_recv.at[which, p, k - 1],
            device_id=near(p, k)[1], device_id_type=MESH)

    def token_copy(c, k):
        return pltpu.make_async_remote_copy(
            tok.at[:, pl.ds(c * n, n)], T.at[c, x], t_send.at[c, k - 1], t_recv.at[c, k - 1],
            device_id=near(0, k)[1], device_id_type=MESH)

    def token_copy_other(p, r, k):
        c = r * 4 + KINDS.index(p)
        return pltpu.make_async_remote_copy(
            tok.at[:, pl.ds(c * n, n)], TO.at[p - 1, r, at[p]],
            to_send.at[p - 1, r, k - 1], to_recv.at[p - 1, r, k - 1],
            device_id=near(p, k)[1], device_id_type=MESH)

    for p in range(3):
        for k in range(1, SIDE):
            meta_copy(0, p, k).start()
            meta_copy(1, p, k).start()
    for r in range(rounds):
        for q, p in enumerate(KINDS):
            for k in range(1, SIDE):
                if p == 0:
                    token_copy(r * 4 + q, k).start()
                else:
                    token_copy_other(p, r, k).start()
    for m in range(pairs):
        for which in range(3):
            weight_copy(which, m).start()

    def meta_here(which, p):
        own_meta(which, p).wait()
        for k in range(1, SIDE):
            meta_copy(which, p, k).wait_recv()

    def table_for(p):
        meta_here(0, p)
        pick_table(p)

    pair = lax.broadcasted_iota(jnp.int32, (2 * GROUP, rows), 0)
    before = (
        lax.broadcasted_iota(jnp.int32, (rows, rows), 0)
        < lax.broadcasted_iota(jnp.int32, (rows, rows), 1)
    ).astype(F32).astype(BF16)
    rho = lax.broadcasted_iota(jnp.int32, (slots, 2 * GROUP), 0)
    col = lax.broadcasted_iota(jnp.int32, (slots, 2 * GROUP), 1)
    half = ((lax.broadcasted_iota(jnp.int32, (slots, lanes), 0) % 8) // 4).astype(F32)

    mine = (lax.broadcasted_iota(jnp.int32, (slots, lanes), 0) % 4) == (
        lax.broadcasted_iota(jnp.int32, (slots, lanes), 1) // rows)

    def slot_tables(p, weighted):
        by_first = jnp.where(p == 2, 2, 64)
        by_second = jnp.where(p == 1, 2, 16)
        base = jnp.where(p == 0, 2 * x, jnp.where(p == 1, 16 * y, 64 * z))
        expert = (
            base + (pair // 16) * by_first + ((pair // 4) % 4) * by_second
            + ((pair // 2) % 2) * 8 + pair % 2)
        spots, weights = [], []
        for s in range(SIDE):
            chosen = jnp.zeros((2 * GROUP, rows), F32)
            weight = jnp.zeros((2 * GROUP, rows), F32)
            for k in range(top):
                hit = jnp.broadcast_to(idv[p, s, k:k + 1, :], (2 * GROUP, rows)) == expert
                chosen = jnp.where(hit, 1.0, chosen)
                if weighted:
                    mix = mixv[p, s, k:k + 1, :].astype(F32) * (1.0 / 256.0)
                    weight = jnp.where(hit, jnp.broadcast_to(mix, (2 * GROUP, rows)), weight)
            rank = jnp.dot(chosen.astype(BF16), before, preferred_element_type=F32)
            spots.append(jnp.where(chosen > 0.5, rank + 1.0, 0.0).astype(BF16))
            weights.append(weight.astype(BF16))
        spot = jnp.concatenate(spots, axis=1)
        weight = jnp.concatenate(weights, axis=1)
        pos, mixes = [], []
        for e in range(2):
            spread = (col == (rho // 8) * 2 + e).astype(F32).astype(BF16)
            found = jnp.dot(spread, spot, preferred_element_type=F32)
            pos.append(jnp.where(mine & (found > 0.5), found - half, -9.0))
            if weighted:
                mixes.append(jnp.dot(spread, weight, preferred_element_type=F32))
        return pos, mixes

    def pick_table(p):
        pos, _ = slot_tables(p, False)
        for g in range(CAP):
            hot = jnp.where(
                (pos[0] == 2.0 * g + 1.0) | (pos[1] == 2.0 * g - 6.0), 1.0, 0.0).astype(BF16)
            for q in range(lanes // 128):
                D[p, g * (lanes // 128) + q] = hot[:, q * 128:(q + 1) * 128]

    def block_copy(p, c, step, h):
        spot, to = far_peer(p, step)
        span = pl.ds(*OUTWARD[h])
        return pltpu.make_async_remote_copy(
            O.at[c, span, spot], X.at[c, span, place(p)], d_send.at[h, c], d_recv.at[h, c],
            device_id=to, device_id_type=MESH)

    def own_block(p, c, h):
        span = pl.ds(*OUTWARD[h])
        return pltpu.make_async_copy(
            O.at[c, span, place(p)], X.at[c, span, place(p)], own_sem.at[h, c])

    def send_blocks(p, c, h):
        for step in steps:
            block_copy(p, c, step, h).start()
        own_block(p, c, h).start()

    def send_rows(r, q):
        p, c = KINDS[q], r * 4 + q
        if p == 0:
            own_tokens(c).wait()
            for k in range(1, SIDE):
                token_copy(c, k).wait_recv()
            tokens = T[c].reshape(lanes, n)
        else:
            own_tokens_other(p, r).wait()
            for k in range(1, SIDE):
                token_copy_other(p, r, k).wait_recv()
            tokens = TO[p - 1, r].reshape(lanes, n)
        cut = lanes // 128
        picks = jnp.concatenate(
            [jnp.concatenate([D[p, g * cut + b] for b in range(cut)], axis=1)
             for g in range(CAP)], axis=0)
        O[c] = jnp.dot(picks, tokens, preferred_element_type=F32).reshape(
            CAP, GROUP, 8, n).astype(BF16)
        send_blocks(p, c, 0)

    def dispatch(r, carry):
        for q in range(4):
            send_rows(r, q)
        return carry

    for q in (0, 1, 3, 2):
        if q < 2 or q == 3:
            table_for(KINDS[q])
        send_rows(0, q)
    lax.fori_loop(1, rounds, dispatch, 0)

    def second_half(r, carry):
        for q, p in enumerate(KINDS):
            send_blocks(p, r * 4 + q, 1)
        return carry

    lax.fori_loop(0, rounds, second_half, 0)
    for r in range(rounds):
        for q, p in enumerate(KINDS):
            if p != 0:
                for k in range(1, SIDE):
                    token_copy(r * 4 + q, k).start()

    for p in range(3):
        meta_here(1, p)

    def sum_table(p, carry):
        pos, mixes = slot_tables(p, True)
        pos_t, mix_t = [v.T for v in pos], [v.T for v in mixes]
        for g in range(CAP):
            block = (jnp.where(pos_t[0] == 2.0 * g + 1.0, mix_t[0], 0.0)
                     + jnp.where(pos_t[1] == 2.0 * g - 6.0, mix_t[1], 0.0)).astype(BF16)
            for b in range(2):
                D[p, pl.ds((2 * g + b) * 2, 2)] = block[:, b * 128:(b + 1) * 128].reshape(
                    2, lanes // 2, 128)
        return carry

    lax.fori_loop(0, 3, sum_table, 0)

    here = lax.broadcasted_iota(jnp.int32, (slots, slots), 0)
    there = lax.broadcasted_iota(jnp.int32, (slots, slots), 1)

    def reorder(p):
        scale = 16 if p == 1 else 64
        low, high = there % 4, (there // scale) % 4
        moved = there + (high - low) + (low - high) * scale
        return (here == moved).astype(F32).astype(BF16)

    def all_but_own(buf, part, sem):
        view = buf.at[pl.ds(*part), pl.ds(0, GROUP - 1)]
        return pltpu.make_async_copy(view, view, sem)

    def back_copy(p, c, step, h):
        spot, to = far_peer(p, step)
        span = pl.ds(*HOMEWARD[h])
        return pltpu.make_async_remote_copy(
            X.at[c, span, spot], Y.at[c, span, place(p)], y_send.at[h, c], y_recv.at[h, c],
            device_id=to, device_id_type=MESH)

    def own_back(p, c, h):
        span = pl.ds(*HOMEWARD[h])
        return pltpu.make_async_copy(
            X.at[c, span, place(p)], Y.at[c, span, place(p)], yown_sem.at[h, c])

    def send_back(p, c, h):
        for step in steps:
            back_copy(p, c, step, h).start()
        own_back(p, c, h).start()

    upper = (lax.broadcasted_iota(jnp.int32, (slots, ff), 0) % 8) // 4

    for e in range(2):
        acc[...] = jnp.zeros_like(acc)

        def up_step(r, carry):
            for b in range(2):
                m = 2 * r + b
                if e == 0:
                    weight_copy(0, m).wait()
                    weight_copy(1, m).wait()
                for q in (2 * b, 2 * b + 1):
                    own_block(KINDS[q], r * 4 + q, e).wait()
                    all_but_own(X.at[r * 4 + q], OUTWARD[e], d_recv.at[e, r * 4 + q]).wait()
                p = KINDS[2 * b + 1]
                c = r * 4 + 2 * b
                mixed = jnp.concatenate(
                    [X[c + 1, 3 * e + g].reshape(slots, n) for g in range(4)], axis=1)
                mixed = jnp.dot(reorder(p), mixed, preferred_element_type=F32).astype(BF16)
                v = jnp.concatenate(
                    [jnp.concatenate(
                        [X[c, 3 * e + g].reshape(slots, n), mixed[:, g * n:(g + 1) * n]], axis=1)
                     for g in range(4)], axis=0)
                acc[:, :ff] += jnp.dot(v, Wg[m, e], preferred_element_type=F32)
                acc[:, ff:] += jnp.dot(v, Wu[m, e], preferred_element_type=F32)
            return carry

        lax.fori_loop(0, rounds, up_step, 0)

        def hidden(g, carry):
            part = pl.ds(pl.multiple_of(g * slots, slots), slots)
            h = silu_product(acc[part, :ff], acc[part, ff:])
            mixed_row = (g == 3 * (1 - e)).astype(jnp.int32)
            keep = mixed_row * (upper - e) * (1 - 2 * e) <= 0
            H[e, part, :] = jnp.where(keep, h, 0.0).astype(BF16)
            return carry

        lax.fori_loop(0, 4, hidden, 0)

        def down_step(r, carry):
            for b in range(2):
                m = 2 * r + b
                c = r * 4 + 2 * b
                if e == 0:
                    weight_copy(2, m).wait()
                    low = jnp.dot(H[0, :3 * slots], Wd[m, 0], preferred_element_type=F32)
                    made = [low[g * slots:(g + 1) * slots] for g in range(3)]
                else:
                    high = jnp.dot(H[1], Wd[m, 1], preferred_element_type=F32)
                    low = jnp.dot(H[0, 3 * slots:], Wd[m, 0], preferred_element_type=F32)
                    made = [low + high[:slots]]
                    made += [high[g * slots:(g + 1) * slots] for g in range(1, 4)]
                first = HOMEWARD[e][0]
                for g, v in enumerate(made):
                    X[c, first + g] = v[:, :n].reshape(GROUP, 8, n).astype(BF16)
                send_back(0, c, e)
                p = KINDS[2 * b + 1]
                mixed = jnp.concatenate([v[:, n:].astype(BF16) for v in made], axis=1)
                mixed = jnp.dot(reorder(p), mixed, preferred_element_type=F32)
                for g in range(len(made)):
                    X[c + 1, first + g] = mixed[:, g * n:(g + 1) * n].reshape(
                        GROUP, 8, n).astype(BF16)
                send_back(p, c + 1, e)
            return carry

        lax.fori_loop(0, rounds, down_step, 0)

    for which in range(3):
        small(which).wait()
    for r in range(rounds):
        for q, p in enumerate(KINDS):
            if p != 0:
                own_tokens(r * 4 + q).wait()
                for k in range(1, SIDE):
                    token_copy(r * 4 + q, k).wait_recv()
    shared[...] = jnp.zeros_like(shared)

    def shared_step(c, carry):
        tokens = T[c].reshape(lanes, n)
        span = pl.ds(pl.multiple_of(c * n, n), n)
        shared[0] += jnp.dot(tokens, Sg[0, span, :], preferred_element_type=F32)
        shared[1] += jnp.dot(tokens, Sg[1, span, :], preferred_element_type=F32)
        scored = tokens.astype(F32) * Gv[span].reshape(1, n).astype(F32)
        for q in range(n // 128):
            shared[2] += scored[:, q * 128:(q + 1) * 128]
        return carry

    lax.fori_loop(0, chunks, shared_step, 0)
    shared_hidden = silu_product(shared[0], shared[1]).astype(BF16)
    score = jnp.broadcast_to(jnp.sum(shared[2], axis=1, keepdims=True), (lanes, 128))
    shared[2] = 1.0 / (1.0 + jnp.exp(-score))

    def shared_part(c):
        span = pl.ds(pl.multiple_of(c * n, n), n)
        scale = jnp.concatenate([shared[2]] * (n // 128), axis=1)
        return scale * jnp.dot(shared_hidden, Sd[:, span], preferred_element_type=F32)

    tall = rows // 8

    def spot_of(c, which, s):
        return O.at[c, 2 * which + s // 2, pl.ds(pl.multiple_of((s % 2) * tall, tall), tall)]

    def taken(ref):
        return ref[...].astype(F32).reshape(rows, n)

    def sum_copy(p, c, k):
        other, to = near(p, k)
        return pltpu.make_async_remote_copy(
            spot_of(c, 0, other), rs_in.at[c, at[p]], r_send.at[c, k - 1], r_recv.at[c, k - 1],
            device_id=to, device_id_type=MESH)

    def shared_copy(m, k):
        other, to = near(0, k)
        return pltpu.make_async_remote_copy(
            spot_of(2 * m + 1, 1, other), sh_in.at[m, x], s_send.at[m, k - 1], s_recv.at[m, k - 1],
            device_id=to, device_id_type=MESH)

    def sent(c, carry):
        for h in range(2):
            all_but_own(O.at[c], OUTWARD[h], d_send.at[h, c]).wait()
        return carry

    lax.fori_loop(0, chunks, sent, 0)

    def shared_sums(m, carry):
        O[2 * m + 1, 2:4] = shared_part(2 * m + 1).reshape(2, GROUP, 8, n).astype(BF16)
        for k in range(1, SIDE):
            shared_copy(m, k).start()
        return carry

    lax.fori_loop(0, pairs, shared_sums, 0)

    def finish(r, carry):
        for q, p in enumerate(KINDS):
            c = r * 4 + q
            for k in range(1, SIDE):
                sum_copy(p, c, k).wait_recv()
            total = taken(spot_of(c, 0, at[p]))
            for k in range(1, SIDE):
                total = total + taken(rs_in.at[c, near(p, k)[0]])
            if p != 0:
                m = c // 2
                for k in range(1, SIDE):
                    shared_copy(m, k).wait_recv()
                total = total + taken(spot_of(c, 1, x))
                for k in range(1, SIDE):
                    total = total + taken(sh_in.at[m, near(0, k)[0]])
            out[:, pl.ds(pl.multiple_of(c * n, n), n)] = total.astype(BF16)
        return carry

    def combine(r, carry):
        for q, p in enumerate(KINDS):
            c = r * 4 + q
            for h in range(2):
                own_back(p, c, h).wait()
                all_but_own(Y.at[c], HOMEWARD[h], y_recv.at[h, c]).wait()
            table = jnp.concatenate(
                [D[p, 2 * b:2 * b + 2].reshape(lanes, 128) for b in range(2 * CAP)], axis=1)
            part = jnp.dot(
                table, Y[c].reshape(CAP * slots, n), preferred_element_type=F32)
            if p == 0:
                part = part + shared_part(c)
            O[c, 0:2] = part.reshape(2, GROUP, 8, n).astype(BF16)
            for k in range(1, SIDE):
                sum_copy(p, c, k).start()
        return carry

    lax.fori_loop(0, rounds, combine, 0)

    lax.fori_loop(0, rounds, finish, 0)

    for p in range(3):
        for k in range(1, SIDE):
            meta_copy(0, p, k).wait_send()
            meta_copy(1, p, k).wait_send()

    def drain(r, carry):
        for q, p in enumerate(KINDS):
            c = r * 4 + q
            for k in range(1, SIDE):
                token_copy(c, k).wait_send()
                sum_copy(p, c, k).wait_send()
                if p != 0:
                    token_copy_other(p, r, k).wait_send()
                    shared_copy(c // 2, k).wait_send()
            for h in range(2):
                all_but_own(X.at[c], HOMEWARD[h], y_send.at[h, c]).wait()
        return carry

    lax.fori_loop(0, rounds, drain, 0)


def on_device(chunks, tokens, expert_ids, combine, w_gate, w_up, w_down, gate_up, down, gate_vec):
    rows, model = tokens.shape
    top = expert_ids.shape[1]
    ff, hid = w_gate.shape[2], down.shape[0]
    n = model // chunks
    slots = GROUP * 8
    lanes = SIDE * rows
    rounds, pairs = chunks // 4, chunks // 2
    near = SIDE - 1
    cfg = (chunks, n, rows, model, ff, hid, top)
    any_spec = pl.BlockSpec(memory_space=pl.ANY)
    dma = pltpu.SemaphoreType.DMA
    return pl.pallas_call(
        functools.partial(kernel, cfg),
        out_shape=jax.ShapeDtypeStruct((rows, model), BF16),
        in_specs=[any_spec] * 9,
        out_specs=pl.BlockSpec(memory_space=pltpu.VMEM),
        scratch_shapes=[
            pltpu.VMEM((chunks, SIDE, rows, n), BF16),
            pltpu.VMEM((2, rounds, SIDE, rows, n), BF16),
            pltpu.VMEM((3, SIDE, top, rows), jnp.int32),
            pltpu.VMEM((3, SIDE, top, rows), jnp.int32),
            pltpu.VMEM((3, 4 * CAP, 256, 128), BF16),
            pltpu.VMEM((chunks, CAP, GROUP, 8, n), BF16),
            pltpu.VMEM((chunks, CAP, GROUP, 8, n), BF16),
            pltpu.VMEM((chunks, CAP, GROUP, 8, n), BF16),
            pltpu.VMEM((pairs, 2, 2 * n, ff), BF16),
            pltpu.VMEM((pairs, 2, 2 * n, ff), BF16),
            pltpu.VMEM((pairs, 2, ff, 2 * n), BF16),
            pltpu.VMEM((4 * slots, 2 * ff), F32),
            pltpu.VMEM((2, 4 * slots, ff), BF16),
            pltpu.VMEM((2, model, hid), BF16),
            pltpu.VMEM((hid, model), BF16),
            pltpu.VMEM((model,), BF16),
            pltpu.VMEM((3, lanes, hid), F32),
            pltpu.VMEM((chunks, SIDE, rows // 8, 8, n), BF16),
            pltpu.VMEM((pairs, SIDE, rows // 8, 8, n), BF16),
            dma((2, 3, near)), dma((2, 3, near)),
            dma((chunks, near)), dma((chunks, near)),
            dma((2, rounds, near)), dma((2, rounds, near)),
            dma((2, chunks)), dma((2, chunks)),
            dma((2, chunks)), dma((2, chunks)),
            dma((chunks, near)), dma((chunks, near)),
            dma((pairs, near)), dma((pairs, near)),
            dma((chunks,)), dma((2, rounds)), dma((3, pairs)),
            dma((2, chunks)), dma((2, chunks)), dma((9,)),
        ],
        compiler_params=pltpu.CompilerParams(
            collective_id=0, has_side_effects=True, vmem_limit_bytes=67043328),
    )(tokens, expert_ids.T, combine.T, w_gate, w_up, w_down, gate_up, down,
      gate_vec)


def solution(mesh, chunks=8):
    return jax.shard_map(
        functools.partial(on_device, chunks),
        mesh=mesh,
        in_specs=(
            P(("wide", "narrow"), None),
            P(("wide", "narrow"), None),
            P(("wide", "narrow"), None),
            P(("wide", "narrow"), None, None),
            P(("wide", "narrow"), None, None),
            P(("wide", "narrow"), None, None),
            P(None, None, "narrow"),
            P("narrow", None),
            P(),
        ),
        out_specs=P(("wide", "narrow"), None),
        check_vma=False,
    )
```
